32 devices in a mesh: grp: 2 (over x), row: 16 (over z, y, core).
Axes of the slice: x: 2, y: 2, z: 4, core: 2. Of those that a mesh axis runs over, the one named last changes fastest.
Arguments:
- coordinates: float32 [3, 65536], P(None, ('grp', 'row')), parts along dimension 1, may hold values from -0.12 to 1.12, as said below
- length_scale: float32 [65536], P(('grp', 'row')), parts along dimension 0, may hold values from 0.05 to 0.4
- probes: bfloat16 [64, 65536], P(None, ('grp', 'row')), parts along dimension 1, may hold values from -6 to 6
- near_ids: int32 [256, 16], P(('grp', 'row')), parts along dimension 0, may hold values from 0 to 127, as said below
- near_count: int32 [256], P(('grp', 'row')), parts along dimension 0, may hold values from 8 to 16
- basis_out: bfloat16 [256, 32, 256], P(('grp', 'row')), parts along dimension 0, may hold values from -1 to 1
- basis_in: bfloat16 [256, 32, 256], P(('grp', 'row')), parts along dimension 0, may hold values from -0.375 to 0.375
Outputs:
- sampled: float32 [64, 65536], P(None, ('grp', 'row')), parts along dimension 1
The draws below stay inside these ranges and needn't reach their ends.
There are 2 independent parts, one for each index of `grp`. The reference program is written for one: setup_inputs(seed, part) draws one part's arguments, and reference() takes and returns one part's arrays. A program takes and returns all parts, laid end to end along the dimension named above; each array names one. Nothing has to cross between parts.
Inputs may be any that keep to these rules, and one draw needn't show every extreme that they name: `coordinates`: points of one block lie within 0.12 of a common center in every coordinate. `near_ids`: row i lists i itself first, then distinct blocks whose index differs from i by at most 8; the slots from near_count[i] on hold i again.
All inputs are finite; a program needn't handle non-finite values.
Results may differ from the reference program's by a relative error of at most 0.00055.
The reference program's roundings to bfloat16 on the way count: a program that leaves them out, or rounds other values in their place, can miss the bound.
Values may be sent and summed in bfloat16 or wider, within the bound.
A program may use at most 64 MiB of HBM per device.

```python
import math
import jax
import jax.numpy as jnp
from jax import lax

B = 256
P_SIZE = 64
R = 32
HALO = 8
NEARMAX = 16
NB = 128
N = 32768


def curve_centers(key):
    total_bits = max((NB - 1).bit_length(), 1)
    blocks = jnp.arange(NB).astype(jnp.int32)
    cells = [jnp.zeros((NB,), jnp.int32) for axis_id in range(3)]
    widths = [1, 1, 1]
    for bit in range(total_bits):
        axis_id = bit % 3
        digit = blocks // 2 ** bit % 2
        cells[axis_id] = cells[axis_id] + digit * widths[axis_id]
        widths[axis_id] = widths[axis_id] * 2
    jitter = jax.random.uniform(key, (NB, 3), jnp.float32, -0.25, 0.25)
    columns = []
    for axis_id in range(3):
        position = (cells[axis_id].astype(jnp.float32) + 0.5 + jitter[:, axis_id]) / float(widths[axis_id])
        columns.append(position)
    return jnp.stack(columns, axis=1)


def draw_coordinates(key, part):
    first_key, second_key = jax.random.split(jax.random.fold_in(key, 3))
    centers = curve_centers(first_key)
    spread = 0.06
    jitter = jax.random.uniform(second_key, (NB, B, 3), jnp.float32, -spread, spread)
    points = centers[:, None, :] + jitter
    return points.reshape(N, 3).T


def near_pattern(key):
    first_key, second_key = jax.random.split(jax.random.fold_in(key, 7))
    offsets = jnp.arange(-HALO, HALO + 1).astype(jnp.int32)
    window = 2 * HALO + 1
    blocks = jnp.arange(NB).astype(jnp.int32)[:, None]
    candidate = blocks + offsets[None, :]
    valid = (candidate >= 0) & (candidate < NB) & (offsets[None, :] != 0)
    scores = jax.random.randint(first_key, (NB, window), 0, 1 << 20) * (window + 1) + jnp.arange(window).astype(jnp.int32)[None, :]
    scores = jnp.where(offsets[None, :] == 0, -1, jnp.where(valid, scores, scores + (1 << 28)))
    order = jnp.argsort(scores, axis=1, stable=True)
    ranked = jnp.take_along_axis(candidate, order, axis=1)[:, :NEARMAX]
    usable = jnp.sum(valid.astype(jnp.int32), axis=1) + 1
    wanted = jax.random.randint(second_key, (NB,), HALO, NEARMAX + 1)
    wanted = jnp.where(jnp.arange(NB) == NB // 2, NEARMAX, wanted)
    counts = jnp.minimum(wanted, usable).astype(jnp.int32)
    listed = jnp.where(jnp.arange(NEARMAX)[None, :] < counts[:, None], ranked, blocks)
    return (listed.astype(jnp.int32), counts)


def draw_near_ids(key, part):
    return near_pattern(key)[0]


def draw_near_count(key, part):
    return near_pattern(key)[1]


def block_scale(own_key, extent, cuts, low, high):
    level = 1.0
    for dim, blocks in cuts:
        draws = jax.random.uniform(jax.random.fold_in(jax.random.fold_in(own_key, 6), dim), (blocks,), jnp.float32, low / len(cuts), high / len(cuts))
        level = level * jnp.repeat(jnp.exp(draws), extent[dim] // blocks).reshape((-1,) + (1,) * (len(extent) - 1 - dim))
    return level


def scatter_about(rng, shape, scale, limit, pieces=(), dtype=jnp.bfloat16):
    entries = scale * jax.random.normal(rng, shape, jnp.float32)
    if pieces:
        entries = entries * block_scale(rng, shape, pieces, -0.22, 0.18)
    return jnp.clip(entries, -limit, limit).astype(dtype)


def setup_inputs(seed: int = 0, part: int = 0) -> dict:
    key_of = jax.random.split(jax.random.key(seed), 8)
    part_keys = jax.random.split(jax.random.fold_in(key_of[7], part), 8)
    return {
        "coordinates": draw_coordinates(jax.random.fold_in(jax.random.fold_in(key_of[7], part), 71), part),
        "length_scale": jnp.clip(jnp.exp(math.log(0.4) - 2.0794415 * jax.random.uniform(part_keys[1], (N,), jnp.float32) ** block_scale(part_keys[1], (N,), ((0, 16),), -0.2, 0.2)), 0.05, 0.4),
        "probes": scatter_about(part_keys[2], (P_SIZE, N), 1.0, 6.0, ((1, 16),)),
        "near_ids": draw_near_ids(jax.random.fold_in(jax.random.fold_in(key_of[7], part), 71), part),
        "near_count": draw_near_count(jax.random.fold_in(jax.random.fold_in(key_of[7], part), 71), part),
        "basis_out": scatter_about(part_keys[5], (NB, R, B), R ** -0.5, 1.0, ((0, 16),)),
        "basis_in": scatter_about(part_keys[6], (NB, R, B), B ** -0.5, 0.375, ((0, 16),)),
    }


def matern(first, second):
    sq_dist = (first[0] - second[0]) * (first[0] - second[0])
    sq_dist = sq_dist + (first[1] - second[1]) * (first[1] - second[1])
    sq_dist = sq_dist + (first[2] - second[2]) * (first[2] - second[2])
    mean_sq = 0.5 * (first[3] * first[3] + second[3] * second[3])
    prefac = (first[3] * second[3] / mean_sq) ** 1.5
    scaled = jnp.sqrt(3.0) * jnp.sqrt(sq_dist / mean_sq)
    return prefac * (1.0 + scaled) * jnp.exp(-scaled)

def reference(coordinates, length_scale, probes, near_ids, near_count, basis_out, basis_in):
    records = jnp.concatenate([coordinates, length_scale[None, :]], axis=0)
    rec_blocks = records.reshape(4, NB, B)
    probe_blocks = probes.reshape(P_SIZE, NB, B)
    slots = jnp.arange(NEARMAX).astype(jnp.int32)

    def one_row(inputs):
        row_ids, row_count, index = inputs
        source = rec_blocks[:, row_ids]
        target = rec_blocks[:, index]
        tiles = matern(source[:, :, :, None], target[:, None, None, :])
        keep = (slots < row_count).astype(jnp.float32)
        tiles = (tiles * keep[:, None, None]).astype(jnp.bfloat16)
        source_probe = probe_blocks[:, row_ids]
        return jnp.einsum('psa,sab->pb', source_probe.astype(jnp.float32), tiles.astype(jnp.float32))
    near = lax.map(one_row, (near_ids, near_count, jnp.arange(NB).astype(jnp.int32)))
    near = jnp.transpose(near, (1, 0, 2))
    folded = jnp.einsum('jkb,pjb->jkp', basis_in.astype(jnp.float32), probe_blocks.astype(jnp.float32))
    folded = folded.astype(jnp.bfloat16).reshape(NB, R * P_SIZE)
    center = lax.optimization_barrier(jnp.mean(rec_blocks, axis=2))
    coupling = matern(center[:, :, None], center[:, None, :])
    every = jnp.arange(NB).astype(jnp.int32)
    is_near = jnp.any(near_ids[:, :, None] == every[None, None, :], axis=1)
    coupling = jnp.where(is_near, 0.0, coupling).astype(jnp.bfloat16)
    summed = jnp.dot(coupling, folded, preferred_element_type=jnp.float32).astype(jnp.bfloat16)
    summed = summed.reshape(NB, R, P_SIZE)
    far = jnp.einsum('ikp,ikb->pib', summed.astype(jnp.float32), basis_out.astype(jnp.float32))
    return (near + far).reshape(P_SIZE, N)
```

```python
import functools
import math

import jax
import jax.numpy as jnp
from jax import lax
from jax.experimental import pallas as pl
from jax.experimental.pallas import tpu as pltpu
from jax.sharding import PartitionSpec as P

HALO = 8
ROWS = 16
CHUNKS = 1
OWN_FIRST = 3
OPEN_AT = 1
LOG2E = 1.0 / math.log(2.0)
C_SCALE = math.log(2.0) ** (-2.0 / 3.0)
D_SCALE = 3.0 * LOG2E * LOG2E * C_SCALE
F32 = jnp.float32
BF16 = jnp.bfloat16


def split3(x):
    high = x.astype(BF16)
    rest = x - high.astype(F32)
    mid = rest.astype(BF16)
    low = (rest - mid.astype(F32)).astype(BF16)
    return high, mid, low


def left_stack(x):
    h, m, l = [part.astype(F32) for part in split3(x)]
    return jnp.concatenate([h, h, m, h, l, m, m, l], axis=0)


def right_stack(x):
    h, m, l = split3(x)
    return jnp.concatenate([h, m, h, l, h, m, l, m], axis=0)


def matern(first, second):
    sq_dist = (first[0] - second[0]) * (first[0] - second[0])
    sq_dist = sq_dist + (first[1] - second[1]) * (first[1] - second[1])
    sq_dist = sq_dist + (first[2] - second[2]) * (first[2] - second[2])
    mean_sq = 0.5 * (first[3] * first[3] + second[3] * second[3])
    ratio = first[3] * second[3] / mean_sq
    prefac = ratio * jnp.sqrt(ratio)
    scaled = jnp.sqrt(3.0 * (sq_dist / mean_sq))
    return prefac * (1.0 + scaled) * jnp.exp(-scaled)


def nt(a, b):
    return lax.dot_general(a, b, (((1,), (1,)), ((), ())), preferred_element_type=F32)


def tn(a, b):
    return lax.dot_general(a, b, (((0,), (0,)), ((), ())), preferred_element_type=F32)


def nn(a, b):
    return lax.dot_general(a, b, (((1,), (0,)), ((), ())), preferred_element_type=F32)


def bit_reverse(x, bits):
    out = x * 0
    for k in range(bits):
        out = out + (x // 2 ** k) % 2 * 2 ** (bits - 1 - k)
    return out


def kernel(
    n, ob, bs,
    xyz_in, len_in, probes_in, ids_in, bout_in, bin_in, out_ref,
    xyz_ref, len_ref, probes_ref, ids_ref, bout_ref, bin_ref,
    xyz_r, len_r, ids_r,
    rec_i, rec_j, cen_j, lhs, rhs_c, mask_a, mask_b, acc, part,
    fold_all, cen_all,
    value_buf, load_sem, halo_send, halo_recv, part_send, part_recv, gat_send, gat_recv, cen_send, cen_recv,
):
    me = lax.axis_index("row")
    bits = n.bit_length() - 1
    own = ob * bs
    left = jnp.maximum(me - 1, 0)
    right = jnp.minimum(me + 1, n - 1)
    has_left = me > 0
    has_right = me < n - 1
    place = bit_reverse(me, bits)
    half = bin_ref.shape[1] // 2
    np_ = probes_ref.shape[0]
    width = n * ob
    own_probes = probes_ref.at[:, 0:own]
    loads = [
        pltpu.make_async_copy(src, dst, load_sem.at[k])
        for k, (src, dst) in enumerate(
            (
                (xyz_in, xyz_ref), (len_in, len_ref), (ids_in, ids_ref),
                (probes_in, own_probes), (bin_in, bin_ref), (bout_in, bout_ref),
            )
        )
    ]
    for load in loads:
        load.start()

    def partner(step):
        bit = 2 ** (bits - 1 - step)
        return me + bit * (1 - 2 * (me // bit % 2))

    barrier = pltpu.get_barrier_semaphore()

    @pl.when(has_left)
    def _():
        pl.semaphore_signal(barrier, inc=1, device_id={"row": left})

    @pl.when(has_right)
    def _():
        pl.semaphore_signal(barrier, inc=1, device_id={"row": right})

    for step in range(bits):
        pl.semaphore_signal(barrier, inc=1, device_id={"row": partner(step)})

    halo = [
        pltpu.make_async_remote_copy(
            src_ref=src, dst_ref=dst, send_sem=halo_send.at[k], recv_sem=halo_recv.at[k], device_id={"row": left}
        )
        for k, (src, dst) in enumerate(
            ((xyz_in, xyz_r), (len_in, len_r), (ids_in, ids_r), (probes_in, probes_ref.at[:, own:]))
        )
    ]

    def gather_copies(step):
        size = 2 ** step
        held = pl.ds(place // size * size, size)
        peer = {"row": partner(step)}
        return (
            pltpu.make_async_remote_copy(
                src_ref=fold_all.at[held], dst_ref=fold_all.at[held],
                send_sem=gat_send.at[step], recv_sem=gat_recv.at[step], device_id=peer,
            ),
            pltpu.make_async_remote_copy(
                src_ref=cen_all.at[held], dst_ref=cen_all.at[held],
                send_sem=cen_send.at[step], recv_sem=cen_recv.at[step], device_id=peer,
            ),
        )

    def gather_start(step):
        for copy in gather_copies(step):
            copy.start()

    def gather_wait(step):
        for copy in gather_copies(step):
            copy.wait()

    def part_copy(col):
        return pltpu.make_async_remote_copy(
            src_ref=acc.at[ob + col], dst_ref=part.at[col],
            send_sem=part_send.at[col], recv_sem=part_recv.at[col], device_id={"row": right},
        )

    for load in loads[:5]:
        load.wait()
    row = lax.broadcasted_iota(jnp.int32, (ROWS, bs), 0)

    def fill_j(xyz, length, base):
        rec_j[0:3, base : base + ob * bs] = xyz[...]
        rec_j[3:6, base : base + ob * bs] = jnp.ones((3, ob * bs), F32)
        rec_j[6:9, base : base + ob * bs] = xyz[...]
        rec_j[9:10, base : base + ob * bs] = jnp.ones((1, ob * bs), F32)
        ln = length[...]
        rec_j[10:11, base : base + ob * bs] = ln * ln
        rec_j[11:12, base : base + ob * bs] = 1.0 / ln
        rec_j[12:16, base : base + ob * bs] = jnp.zeros((4, ob * bs), F32)
        for b in range(ob):
            at = base + b * bs
            blk = rec_j[:, at : at + bs]
            inv = rec_j[11:12, at : at + bs]
            feat = jnp.where((row == 9) | (row == 10), blk, 0.0) * (inv * (0.5 * C_SCALE))
            rhs_c[base // bs + b] = right_stack(feat)

    rec_i[0:3, :] = xyz_ref[...]
    rec_i[3:6, :] = xyz_ref[...]
    rec_i[6:9, :] = jnp.ones((3, ob * bs), F32)
    ln0 = len_ref[...]
    rec_i[9:10, :] = ln0 * ln0
    rec_i[10:11, :] = jnp.ones((1, ob * bs), F32)
    rec_i[11:12, :] = ln0
    rec_i[12:16, :] = jnp.zeros((4, ob * bs), F32)
    fill_j(xyz_ref, len_ref, 0)

    lane = lax.broadcasted_iota(jnp.int32, (ROWS, 128), 1)
    own_centers = jnp.zeros((ROWS, 128), F32)
    for b in range(ob):
        blk = rec_i[:, b * bs : (b + 1) * bs]
        mean = jnp.sum(blk, axis=1, keepdims=True) * (1.0 / bs)
        own_centers = jnp.where(lane == b, mean, own_centers)
        mean_w = jnp.broadcast_to(mean, (ROWS, bs))
        cen = jnp.where(row < 6, mean_w, 0.0)
        v = blk - cen
        feat = jnp.where((row >= 3) & (row < 6), v * v, jnp.where(row < 11, v, 0.0)) * (1.0 / rec_i[11:12, b * bs : (b + 1) * bs])
        lhs[b] = left_stack(feat).T.astype(BF16)
        mean_j = jnp.sum(rec_j[:, b * bs : (b + 1) * bs], axis=1, keepdims=True) * (1.0 / bs)
        cen_j[b] = jnp.where((row < 3) | ((row >= 6) & (row < 9)), jnp.broadcast_to(mean_j, (ROWS, bs)), 0.0)
        pb = probes_ref[:, b * bs : (b + 1) * bs]
        fold = jnp.concatenate([nt(bin_ref[b, 0:half, :], pb), nt(bin_ref[b, half:, :], pb)], axis=1)
        fold_all[place, b * half : (b + 1) * half, :] = fold.astype(BF16)
    square = jnp.concatenate([own_centers, jnp.zeros((128 - ROWS, 128), F32)], axis=0).T
    own_cols = square[0:ob, :]
    cen_all[place] = own_cols

    acc[...] = jnp.zeros_like(acc)

    def member(ids, target):
        return jnp.max(jnp.where(ids == target, 1.0, 0.0), axis=1, keepdims=True)

    def store_rows(ref, base, value):
        wide = jnp.broadcast_to(value, (ob, bs))
        for b in range(ob):
            ref[base + b] = wide[b : b + 1, :]

    ids = ids_ref[...]
    gid = lax.broadcasted_iota(jnp.int32, ids.shape, 0) + me * ob
    for dj in range(HALO + 1):
        store_rows(mask_a, dj * ob, member(ids, gid + dj))
        if dj:
            store_rows(mask_b, dj * 2 * ob, member(ids, gid - dj))
        else:
            store_rows(mask_b, 0, jnp.zeros((ob, 1), F32))

    rows = bs // CHUNKS

    def right_side(i, jw):
        at = pl.multiple_of(jw * bs, bs)
        v = rec_j[:, pl.ds(at, bs)] - cen_j[i]
        feat = jnp.where(
            row < 3, (-2.0 * D_SCALE) * v,
            jnp.where(row < 6, D_SCALE, jnp.where(row < 9, D_SCALE * v * v, 0.0)),
        ) * rec_j[11:12, pl.ds(at, bs)]
        return jnp.concatenate([right_stack(feat), rhs_c[jw]], axis=1)

    def entries(i, side, c):
        return nn(lhs[i, c * rows : (c + 1) * rows, :], side)

    def values(both):
        w = lax.rsqrt(both[:, bs:])
        w2 = w * w
        u = jnp.maximum(both[:, :bs] * w2, 1e-30)
        s = u * lax.rsqrt(u)
        return (((w2 * w) * (LOG2E + s)) * jnp.exp2(-s)).astype(BF16)

    def products(i, jw, slot):
        dj = jw - i
        value = value_buf[slot]
        p_j = probes_ref[:, pl.ds(pl.multiple_of(jw * bs, bs), bs)]
        p_i = probes_ref[:, pl.ds(pl.multiple_of(i * bs, bs), bs)]
        acc[i] += mask_a[dj * ob + i] * nt(p_j, value)
        acc[jw] += mask_b[dj * 2 * ob + jw] * nn(p_i, value)

    def sweep(pairs):
        side = right_side(*pairs[0])
        current = [entries(pairs[0][0], side, c) for c in range(CHUNKS)]
        for t, (i, jw) in enumerate(pairs):
            upcoming = None
            if t + 1 < len(pairs):
                upcoming = right_side(*pairs[t + 1])
            following = []
            for c in range(CHUNKS):
                if upcoming is not None:
                    following.append(entries(pairs[t + 1][0], upcoming, c))
                value_buf[t % 2, c * rows : (c + 1) * rows, :] = values(current[c])
                if c == 0 and t:
                    products(*pairs[t - 1], (t - 1) % 2)
            current = following
        last = len(pairs) - 1
        products(*pairs[last], last % 2)

    def triangle(g, s):
        c = (s + g) // ob
        a = g + c * (ob - 1 - 2 * g)
        return a, a + s - c * (ob - g)

    groups = ob // 2
    ahead = min(OWN_FIRST, groups)

    def open_links():
        pl.semaphore_wait(barrier, bits + jnp.where(has_left, 1, 0) + jnp.where(has_right, 1, 0))

        @pl.when(has_left)
        def _():
            for copy in halo:
                copy.start()

        gather_start(0)

    def take_halo():
        @pl.when(has_right)
        def _():
            for copy in halo:
                copy.wait_recv()

        @pl.when(jnp.logical_not(has_right))
        def _():
            xyz_r[...] = xyz_ref[...]
            len_r[...] = len_ref[...]
            ids_r[...] = ids_ref[...]
            probes_ref[:, own:] = probes_ref[:, 0:own]

        fill_j(xyz_r, len_r, own)
        ids2 = ids_r[...]
        for dj in range(1, HALO + 1):
            store_rows(mask_b, dj * 2 * ob + ob, member(ids2, gid + ob - dj))

    def advance(step):
        gather_wait(step - 1)
        gather_start(step)

    hooks = [(OPEN_AT, open_links), (ahead, take_halo)]
    for step in range(1, bits):
        hooks.append((min(OPEN_AT + 1 + step, 2 * groups - 1), functools.partial(advance, step)))

    def group(t, carry):
        for at, hook in hooks:
            pl.when(t == at)(hook)
        cross = jnp.logical_and(t >= ahead, t < ahead + groups)
        g = t - jnp.where(t < ahead, 0, jnp.where(cross, ahead, groups))
        pairs = []
        for s in range(ob + 1):
            a, b = triangle(g, s)
            pairs.append((jnp.where(cross, b, a), jnp.where(cross, ob + a, b)))
        sweep(pairs)

        @pl.when(jnp.logical_and(cross, has_right))
        def _():
            part_copy(g).start()
            part_copy(ob - 1 - g).start()

        return carry

    lax.fori_loop(0, 2 * groups, group, 0)

    gather_wait(bits - 1)
    centers = cen_all[...].reshape(width, 128).T
    picks = (0, 1, 2, 11)
    coupling = matern([own_cols[:, c : c + 1] for c in picks], [centers[c : c + 1, :] for c in picks])
    column = lax.broadcasted_iota(jnp.int32, (ob, width), 1)
    global_ids = bit_reverse(column // ob, bits) * ob + column % ob
    near = jnp.zeros((ob, width), F32)
    for t in range(ids.shape[1]):
        near = jnp.where(ids[:, t : t + 1] == global_ids, 1.0, near)
    coupling = jnp.where(near > 0.0, 0.0, coupling).astype(BF16)

    step_w = 128
    total = jnp.zeros((ob * half, 2 * np_), F32)
    pick_r = lax.broadcasted_iota(jnp.int32, (step_w, step_w * half), 0)
    pick_c = lax.broadcasted_iota(jnp.int32, (step_w, step_w * half), 1)
    spread = jnp.where(pick_c // half == pick_r, 1.0, 0.0).astype(BF16)
    eye_r = lax.broadcasted_iota(jnp.int32, (ob * half, step_w * half), 0)
    eye_c = lax.broadcasted_iota(jnp.int32, (ob * half, step_w * half), 1)
    same = lax.rem(eye_r, half) == lax.rem(eye_c, half)
    per = step_w // ob
    for q in range(width // step_w):
        wide = nn(coupling[:, q * step_w : (q + 1) * step_w], spread)
        wide = jnp.concatenate(
            [jnp.broadcast_to(wide[i : i + 1, :], (half, step_w * half)) for i in range(ob)], axis=0
        )
        kron = jnp.where(same, wide, 0.0).astype(BF16)
        folded = fold_all[q * per : (q + 1) * per].reshape(step_w * half, 2 * np_)
        total = total + nn(kron, folded)
    summed = total.astype(BF16)

    loads[5].wait()

    @pl.when(has_left)
    def _():
        for copy in halo:
            copy.wait_send()
        for b in range(ob):
            part_copy(b).wait_recv()

    @pl.when(jnp.logical_not(has_left))
    def _():
        part[...] = jnp.zeros_like(part)

    for b in range(ob):
        mine = summed[b * half : (b + 1) * half, :]
        far = tn(mine[:, :np_], bout_ref[b, 0:half, :]) + tn(mine[:, np_:], bout_ref[b, half:, :])
        out_ref[:, b * bs : (b + 1) * bs] = acc[b] + part[b] + far

    @pl.when(has_right)
    def _():
        for b in range(ob):
            part_copy(b).wait_send()


def solution(mesh):
    n = mesh.shape["row"]

    def shards(coordinates, length_scale, probes, near_ids, near_count, basis_out, basis_in):
        ob, rank, bs = basis_out.shape
        np_ = probes.shape[0]
        own = ob * bs
        slots = near_ids.shape[1]
        vmem = pl.BlockSpec(memory_space=pltpu.VMEM)
        dma = pltpu.SemaphoreType.DMA
        return pl.pallas_call(
            functools.partial(kernel, n, ob, bs),
            out_shape=jax.ShapeDtypeStruct((np_, own), F32),
            in_specs=[pl.BlockSpec(memory_space=pl.ANY)] * 6,
            out_specs=vmem,
            scratch_shapes=[
                pltpu.VMEM((3, own), F32),
                pltpu.VMEM((1, own), F32),
                pltpu.VMEM((np_, 2 * own), BF16),
                pltpu.VMEM((ob, slots), jnp.int32),
                pltpu.VMEM((ob, rank, bs), BF16),
                pltpu.VMEM((ob, rank, bs), BF16),
                pltpu.VMEM((3, own), F32),
                pltpu.VMEM((1, own), F32),
                pltpu.VMEM((ob, slots), jnp.int32),
                pltpu.VMEM((ROWS, own), F32),
                pltpu.VMEM((ROWS, 2 * own), F32),
                pltpu.VMEM((ob, ROWS, bs), F32),
                pltpu.VMEM((ob, bs, 8 * ROWS), BF16),
                pltpu.VMEM((2 * ob, 8 * ROWS, bs), BF16),
                pltpu.VMEM(((HALO + 1) * ob, 1, bs), F32),
                pltpu.VMEM(((HALO + 1) * 2 * ob, 1, bs), F32),
                pltpu.VMEM((2 * ob, np_, bs), F32),
                pltpu.VMEM((ob, np_, bs), F32),
                pltpu.VMEM((n, ob * rank // 2, 2 * np_), BF16),
                pltpu.VMEM((n, ob, 128), F32),
                pltpu.VMEM((2, bs, bs), BF16),
                dma((6,)), dma((4,)), dma((4,)), dma((ob,)), dma((ob,)),
                dma((n,)), dma((n,)), dma((n,)), dma((n,)),
            ],
            compiler_params=pltpu.CompilerParams(collective_id=0, has_side_effects=True, vmem_limit_bytes=60 * 1024 * 1024),
        )(coordinates, length_scale.reshape(1, own), probes, near_ids, basis_out, basis_in)

    placed = (
        P(None, ("grp", "row")),
        P(("grp", "row")),
        P(None, ("grp", "row")),
        P(("grp", "row"), None),
        P(("grp", "row")),
        P(("grp", "row"), None, None),
        P(("grp", "row"), None, None),
    )
    return jax.shard_map(
        shards, mesh=mesh, in_specs=placed, out_specs=P(None, ("grp", "row")), check_vma=False
    )
```

```python
import functools
import math

import jax
import jax.numpy as jnp
from jax import lax
from jax.experimental import pallas as pl
from jax.experimental.pallas import tpu as pltpu
from jax.sharding import PartitionSpec as P

HALO = 8
ROWS = 16
OPEN_AT = 1
LEVEL_AT = 8
LOG2E = 1.0 / math.log(2.0)
C_SCALE = math.log(2.0) ** (-2.0 / 3.0)
D_SCALE = 3.0 * LOG2E * LOG2E * C_SCALE
F32 = jnp.float32
BF16 = jnp.bfloat16


def split3(x):
    high = x.astype(BF16)
    rest = x - high.astype(F32)
    mid = rest.astype(BF16)
    low = (rest - mid.astype(F32)).astype(BF16)
    return high, mid, low


def left_stack(x):
    h, m, l = [part.astype(F32) for part in split3(x)]
    return jnp.concatenate([h, h, m, h, l, m, m, l], axis=0)


def right_stack(x):
    h, m, l = split3(x)
    return jnp.concatenate([h, m, h, l, h, m, l, m], axis=0)


def matern(first, second):
    sq_dist = (first[0] - second[0]) * (first[0] - second[0])
    sq_dist = sq_dist + (first[1] - second[1]) * (first[1] - second[1])
    sq_dist = sq_dist + (first[2] - second[2]) * (first[2] - second[2])
    mean_sq = 0.5 * (first[3] * first[3] + second[3] * second[3])
    ratio = first[3] * second[3] / mean_sq
    prefac = ratio * jnp.sqrt(ratio)
    scaled = jnp.sqrt(3.0 * (sq_dist / mean_sq))
    return prefac * (1.0 + scaled) * jnp.exp(-scaled)


def nt(a, b):
    return lax.dot_general(a, b, (((1,), (1,)), ((), ())), preferred_element_type=F32)


def tn(a, b):
    return lax.dot_general(a, b, (((0,), (0,)), ((), ())), preferred_element_type=F32)


def nn(a, b):
    return lax.dot_general(a, b, (((1,), (0,)), ((), ())), preferred_element_type=F32)


def kernel(
    n, ob, bs,
    xyz_in, len_in, probes_in, ids_in, bout_in, bin_in, out_ref,
    xyz_ref, len_ref, ids_ref, bout_ref, bin_ref,
    xyz_h, len_h, ids_h, probes,
    rec_i, rec_j, cen_j, lhs, rhs_c, mask, acc, part,
    fold_all, cen_all, cen_y, red_out, red_in,
    value_buf, load_sem, halo_send, halo_recv, part_send, part_recv,
    gat_send, gat_recv, cen_send, cen_recv, low_send, low_recv,
):
    me = lax.axis_index("row")
    own = ob * bs
    h = ob // 2
    window = ob + 2 * h
    hb = h * bs
    quads = n // 4
    core = me % 2
    col_y = me // 2 % 2
    hi = me // 4
    fast = me + 1 - 2 * core
    slow = jnp.clip(me - 1 + 2 * core, 0, n - 1)
    has_left = me > 0
    has_right = me < n - 1
    has_slow = jnp.where(core == 0, has_left, has_right)
    across = me + 2 - 4 * col_y
    side_fast = 1 - core
    side_slow = core
    half = bin_ref.shape[1] // 2
    np_ = probes.shape[0]
    width = n // 2 * ob

    loads = [
        pltpu.make_async_copy(src, dst, load_sem.at[k])
        for k, (src, dst) in enumerate(
            (
                (xyz_in, xyz_ref), (len_in, len_ref), (ids_in, ids_ref),
                (probes_in, probes.at[:, hb : hb + own]), (bin_in, bin_ref), (bout_in, bout_ref),
            )
        )
    ]
    for load in loads:
        load.start()

    barrier = pltpu.get_barrier_semaphore()

    def greet(peer):
        pl.semaphore_signal(barrier, inc=1, device_id={"row": peer})

    greet(fast)
    pl.when(has_slow)(lambda: greet(slow))
    greet(across)

    def level(k):
        return lax.rem(hi + k, quads) * 4 + me % 4

    for k in range(1, quads):
        greet(level(k))

    def lanes(start, size):
        return pl.ds(pl.multiple_of(start, size), size)

    def halo_out(side, peer):
        src = lanes(side * hb, hb)
        there = 1 - side
        pairs = (
            (xyz_in.at[:, src], xyz_h.at[there]),
            (len_in.at[:, src], len_h.at[there]),
            (ids_in, ids_h.at[there]),
            (probes_in.at[:, src], probes.at[:, lanes(there * (own + hb), hb)]),
        )
        return [
            pltpu.make_async_remote_copy(
                src_ref=a, dst_ref=b, send_sem=halo_send.at[side, k], recv_sem=halo_recv.at[there, k],
                device_id={"row": peer},
            )
            for k, (a, b) in enumerate(pairs)
        ]

    def halo_arrival(side, peer):
        pairs = (
            (xyz_in.at[:, 0:hb], xyz_h.at[side]),
            (len_in.at[:, 0:hb], len_h.at[side]),
            (ids_in, ids_h.at[side]),
            (probes_in.at[:, 0:hb], probes.at[:, lanes(side * (own + hb), hb)]),
        )
        return [
            pltpu.make_async_remote_copy(
                src_ref=a, dst_ref=b, send_sem=halo_send.at[side, k], recv_sem=halo_recv.at[side, k],
                device_id={"row": peer},
            )
            for k, (a, b) in enumerate(pairs)
        ]

    slot = core * quads + hi

    def level_copies(k, source):
        at = core * quads + source
        return [
            pltpu.make_async_remote_copy(
                src_ref=fold_all.at[at], dst_ref=fold_all.at[at],
                send_sem=gat_send.at[k], recv_sem=gat_recv.at[k], device_id={"row": level(k)},
            ),
            pltpu.make_async_remote_copy(
                src_ref=cen_all.at[at], dst_ref=cen_all.at[at],
                send_sem=cen_send.at[k], recv_sem=cen_recv.at[k], device_id={"row": level(k)},
            ),
        ]

    def core_copies(which):
        held = pl.ds(which * quads, quads)
        return [
            pltpu.make_async_remote_copy(
                src_ref=fold_all.at[held], dst_ref=fold_all.at[held],
                send_sem=low_send.at[0], recv_sem=low_recv.at[0], device_id={"row": fast},
            ),
            pltpu.make_async_remote_copy(
                src_ref=cen_all.at[held], dst_ref=cen_all.at[held],
                send_sem=low_send.at[1], recv_sem=low_recv.at[1], device_id={"row": fast},
            ),
        ]

    center_copy = pltpu.make_async_remote_copy(
        src_ref=cen_all.at[slot], dst_ref=cen_y,
        send_sem=low_send.at[2], recv_sem=low_recv.at[2], device_id={"row": across},
    )
    sum_copy = pltpu.make_async_remote_copy(
        src_ref=red_out, dst_ref=red_in,
        send_sem=low_send.at[3], recv_sem=low_recv.at[3], device_id={"row": across},
    )

    def part_copy(side, x, peer):
        return pltpu.make_async_remote_copy(
            src_ref=acc.at[(ob + h) * side + x], dst_ref=part.at[h * (1 - side) + x],
            send_sem=part_send.at[side * h + x], recv_sem=part_recv.at[h * (1 - side) + x],
            device_id={"row": peer},
        )

    def part_arrival(b, peer):
        return pltpu.make_async_remote_copy(
            src_ref=acc.at[b], dst_ref=part.at[b],
            send_sem=part_send.at[b], recv_sem=part_recv.at[b], device_id={"row": peer},
        )

    for load in loads[:5]:
        load.wait()
    row = lax.broadcasted_iota(jnp.int32, (ROWS, bs), 0)

    def fill_j(at, xyz, ln):
        rec_j[at, 0:3, :] = xyz
        rec_j[at, 3:6, :] = jnp.ones((3, bs), F32)
        rec_j[at, 6:9, :] = xyz
        rec_j[at, 9:10, :] = jnp.ones((1, bs), F32)
        rec_j[at, 10:11, :] = ln * ln
        rec_j[at, 11:12, :] = 1.0 / ln
        rec_j[at, 12:16, :] = jnp.zeros((4, bs), F32)
        feat = jnp.where((row == 9) | (row == 10), rec_j[at], 0.0) * (rec_j[at, 11:12, :] * (0.5 * C_SCALE))
        rhs_c[at] = right_stack(feat)

    rec_i[0:3, :] = xyz_ref[...]
    rec_i[3:6, :] = xyz_ref[...]
    rec_i[6:9, :] = jnp.ones((3, own), F32)
    ln0 = len_ref[...]
    rec_i[9:10, :] = ln0 * ln0
    rec_i[10:11, :] = jnp.ones((1, own), F32)
    rec_i[11:12, :] = ln0
    rec_i[12:16, :] = jnp.zeros((4, own), F32)

    ids = ids_ref[...]
    slots = ids.shape[1]
    lane = lax.broadcasted_iota(jnp.int32, (ROWS, 128), 1)
    own_centers = jnp.zeros((ROWS, 128), F32)
    for b in range(ob):
        blk = rec_i[:, b * bs : (b + 1) * bs]
        mean = jnp.sum(blk, axis=1, keepdims=True) * (1.0 / bs)
        own_centers = jnp.where(lane == b, mean, own_centers)
        mean_w = jnp.broadcast_to(mean, (ROWS, bs))
        cen = jnp.where(row < 6, mean_w, 0.0)
        v = blk - cen
        feat = jnp.where((row >= 3) & (row < 6), v * v, jnp.where(row < 11, v, 0.0)) * (1.0 / rec_i[11:12, b * bs : (b + 1) * bs])
        lhs[b] = left_stack(feat).T.astype(BF16)
        fill_j(h + b, xyz_ref[:, b * bs : (b + 1) * bs], len_ref[:, b * bs : (b + 1) * bs])
        mean_j = jnp.sum(rec_j[h + b], axis=1, keepdims=True) * (1.0 / bs)
        cen_j[b] = jnp.where((row < 3) | ((row >= 6) & (row < 9)), jnp.broadcast_to(mean_j, (ROWS, bs)), 0.0)
        pb = probes[:, hb + b * bs : hb + (b + 1) * bs]
        fold = jnp.concatenate([nt(bin_ref[b, 0:half, :], pb), nt(bin_ref[b, half:, :], pb)], axis=1)
        fold_all[slot, b * half : (b + 1) * half, :] = fold.astype(BF16)
    square = jnp.concatenate([own_centers, jnp.zeros((128 - ROWS, 128), F32)], axis=0).T
    id_rows = jnp.concatenate(
        [jnp.zeros((ob, ROWS), F32), ids.astype(F32), jnp.zeros((ob, 128 - ROWS - slots), F32)], axis=1
    )
    own_cols = square[0:ob, :] + id_rows
    cen_all[slot] = own_cols

    acc[...] = jnp.zeros_like(acc)

    def member(ids, target):
        return jnp.max(jnp.where(ids == target, 1.0, 0.0), axis=1, keepdims=True)

    gid = lax.broadcasted_iota(jnp.int32, ids.shape, 0) + me * ob

    def mask_at(offset, q):
        return (offset + HALO) * window + q

    for offset in range(-HALO, HALO + 1):
        wide = jnp.broadcast_to(member(ids, gid + offset), (ob, bs))
        for b in range(ob):
            mask[mask_at(offset, h + b)] = wide[b : b + 1, :]
    blank = (2 * HALO + 1) * window
    mask[blank] = jnp.zeros((1, bs), F32)

    def right_side(o, q):
        v = rec_j[q] - cen_j[o]
        feat = jnp.where(
            row < 3, (-2.0 * D_SCALE) * v,
            jnp.where(row < 6, D_SCALE, jnp.where(row < 9, D_SCALE * v * v, 0.0)),
        ) * rec_j[q, 11:12, :]
        return jnp.concatenate([right_stack(feat), rhs_c[q]], axis=1)

    def values(both):
        w = lax.rsqrt(both[:, bs:])
        w2 = w * w
        u = jnp.maximum(both[:, :bs] * w2, 1e-30)
        s = u * lax.rsqrt(u)
        return (((w2 * w) * (LOG2E + s)) * jnp.exp2(-s)).astype(BF16)

    def products(o, q, turn):
        offset = q - h - o
        value = value_buf[turn]
        p_q = probes[:, lanes(q * bs, bs)]
        p_o = probes[:, lanes((h + o) * bs, bs)]
        acc[h + o] += mask[mask_at(offset, h + o)] * nt(p_q, value)
        acc[q] += mask[jnp.where(offset == 0, blank, mask_at(-offset, q))] * nn(p_o, value)

    def sweep(pairs):
        current = nn(lhs[pairs[0][0]], right_side(*pairs[0]))
        for t, pair in enumerate(pairs):
            if t + 1 < len(pairs):
                following = nn(lhs[pairs[t + 1][0]], right_side(*pairs[t + 1]))
            value_buf[t % 2] = values(current)
            if t:
                products(*pairs[t - 1], (t - 1) % 2)
            current = following
        products(*pairs[-1], (len(pairs) - 1) % 2)

    table = []
    for g in range(h):
        c = [(s + g) // ob for s in range(ob + 1)]
        first = [g + k * (ob - 1 - 2 * g) for k in c]
        table.append([(f, h + f + s - k * (ob - g)) for s, (k, f) in enumerate(zip(c, first))])
    for g in range(h // 2):
        cols = [(g, ob), (h - 1 - g, h)]
        table.append([(i, h + ob + c) for c, stop in cols for i in range(c, stop)])
    for g in range(h // 2):
        table.append([(c, i - h) for i in (h + g, ob - 1 - g) for c in range(h // 2, i + 1)])

    def pick(kind, entries):
        out = jnp.int32(entries[0])
        for k in range(1, len(entries)):
            if entries[k] != entries[0]:
                out = jnp.where(kind == k, entries[k], out)
        return out

    def open_links():
        pl.semaphore_wait(barrier, quads + 1 + jnp.where(has_slow, 1, 0))

        @pl.when(has_slow)
        def _():
            for copy in halo_out(side_slow, slow):
                copy.start()

        for copy in halo_out(side_fast, fast):
            copy.start()
        for k in range(1, quads):
            for copy in level_copies(k, hi):
                copy.start()
        center_copy.start()

    def take_halo(side):
        first = side * (ob + h)
        for b in range(h):
            fill_j(first + b, xyz_h[side, :, b * bs : (b + 1) * bs], len_h[side, :, b * bs : (b + 1) * bs])
        there = ids_h[side]
        sign = 1 - 2 * side
        base = gid + (2 * side - 1) * ob
        for dj in range(1, HALO + 1):
            wide = jnp.broadcast_to(member(there, base + sign * dj), (ob, bs))
            part_rows = jnp.where(side == 0, wide[h:, :], wide[:h, :])
            for b in range(h):
                mask[mask_at(sign * dj, first + b)] = part_rows[b : b + 1, :]

    def take_fast():
        for copy in halo_arrival(side_fast, fast):
            copy.wait_recv()
        take_halo(side_fast)

    def take_slow():
        @pl.when(has_slow)
        def _():
            for copy in halo_arrival(side_slow, slow):
                copy.wait_recv()

        @pl.when(jnp.logical_not(has_slow))
        def _():
            xyz_h[side_slow] = xyz_ref[:, 0:hb]
            len_h[side_slow] = len_ref[:, 0:hb]
            ids_h[side_slow] = ids_ref[...]
            probes[:, lanes(side_slow * (own + hb), hb)] = probes[:, hb : 2 * hb]

        take_halo(side_slow)

    def level_done():
        for k in range(1, quads):
            for copy in level_copies(k, hi):
                copy.wait()
        for copy in core_copies(core):
            copy.start()

    step_w = min(128, width)

    def partial_sums():
        for copy in core_copies(core):
            copy.wait()
        center_copy.wait()
        centers = cen_all[...].reshape(width, 128).T
        mine = cen_all[slot]
        column = lax.broadcasted_iota(jnp.int32, (ob, width), 1)
        holder = column // ob
        device = holder % quads * 4 + col_y * 2 + holder // quads
        global_ids = (device * ob + column % ob).astype(F32)
        picks = (0, 1, 2, 11)
        pick_r = lax.broadcasted_iota(jnp.int32, (step_w, step_w * half), 0)
        pick_c = lax.broadcasted_iota(jnp.int32, (step_w, step_w * half), 1)
        spread = jnp.where(pick_c // half == pick_r, 1.0, 0.0).astype(BF16)
        eye_r = lax.broadcasted_iota(jnp.int32, (ob * half, step_w * half), 0)
        eye_c = lax.broadcasted_iota(jnp.int32, (ob * half, step_w * half), 1)
        same = lax.rem(eye_r, half) == lax.rem(eye_c, half)
        per = step_w // ob
        totals = []
        for rows in (mine, cen_y[...]):
            coupling = matern([rows[:, c : c + 1] for c in picks], [centers[c : c + 1, :] for c in picks])
            near = jnp.zeros((ob, width), F32)
            for t in range(slots):
                near = jnp.where(rows[:, ROWS + t : ROWS + t + 1] == global_ids, 1.0, near)
            coupling = jnp.where(near > 0.0, 0.0, coupling).astype(BF16)
            total = jnp.zeros((ob * half, 2 * np_), F32)
            for q in range(width // step_w):
                wide = nn(coupling[:, q * step_w : (q + 1) * step_w], spread)
                wide = jnp.concatenate(
                    [jnp.broadcast_to(wide[i : i + 1, :], (half, step_w * half)) for i in range(ob)], axis=0
                )
                kron = jnp.where(same, wide, 0.0).astype(BF16)
                folded = fold_all[q * per : (q + 1) * per].reshape(step_w * half, 2 * np_)
                total = total + nn(kron, folded)
            totals.append(total)
        red_out[...] = totals[1]
        sum_copy.start()
        return totals[0]

    hooks = [(OPEN_AT, open_links), (h, take_fast), (h + h // 2, take_slow)]
    if LEVEL_AT < ob:
        hooks.append((LEVEL_AT, level_done))

    def group(t, carry):
        for at, hook in hooks:
            pl.when(t == at)(hook)
        crossing = t >= h
        kind = jnp.where(crossing, h + (t - h + core * (h // 2)) % h, t)
        sweep(
            [
                (pick(kind, [tiles[s][0] for tiles in table]), pick(kind, [tiles[s][1] for tiles in table]))
                for s in range(ob + 1)
            ]
        )
        g = (kind - h) % (h // 2)
        side = jnp.where(kind < h + h // 2, 1, 0)
        is_fast = t < h + h // 2
        peer = jnp.where(is_fast, fast, slow)

        @pl.when(jnp.logical_and(crossing, jnp.logical_or(is_fast, has_slow)))
        def _():
            part_copy(side, g, peer).start()
            part_copy(side, h - 1 - g, peer).start()

        return carry

    lax.fori_loop(0, ob, group, 0)

    if LEVEL_AT >= ob:
        level_done()
    own_sum = partial_sums()
    loads[5].wait()

    for x in range(h):
        part_arrival(side_fast * h + x, fast).wait_recv()

    @pl.when(has_slow)
    def _():
        for x in range(h):
            part_arrival(side_slow * h + x, slow).wait_recv()

    @pl.when(jnp.logical_not(has_slow))
    def _():
        for x in range(h):
            part[side_slow * h + x] = jnp.zeros((np_, bs), F32)

    sum_copy.wait()
    summed = (own_sum + red_in[...]).astype(BF16)
    for b in range(ob):
        mine = summed[b * half : (b + 1) * half, :]
        far = tn(mine[:, :np_], bout_ref[b, 0:half, :]) + tn(mine[:, np_:], bout_ref[b, half:, :])
        out_ref[:, b * bs : (b + 1) * bs] = acc[h + b] + part[b] + far

    for copy in halo_out(side_fast, fast):
        copy.wait_send()
    for x in range(h):
        part_copy(side_fast, x, fast).wait_send()

    @pl.when(has_slow)
    def _():
        for copy in halo_out(side_slow, slow):
            copy.wait_send()
        for x in range(h):
            part_copy(side_slow, x, slow).wait_send()


def solution(mesh):
    n = mesh.shape["row"]

    def shards(coordinates, length_scale, probes, near_ids, near_count, basis_out, basis_in):
        ob, rank, bs = basis_out.shape
        np_ = probes.shape[0]
        own = ob * bs
        h = ob // 2
        slots = near_ids.shape[1]
        window = ob + 2 * h
        vmem = pl.BlockSpec(memory_space=pltpu.VMEM)
        dma = pltpu.SemaphoreType.DMA
        return pl.pallas_call(
            functools.partial(kernel, n, ob, bs),
            out_shape=jax.ShapeDtypeStruct((np_, own), F32),
            in_specs=[pl.BlockSpec(memory_space=pl.ANY)] * 6,
            out_specs=vmem,
            scratch_shapes=[
                pltpu.VMEM((3, own), F32),
                pltpu.VMEM((1, own), F32),
                pltpu.VMEM((ob, slots), jnp.int32),
                pltpu.VMEM((ob, rank, bs), BF16),
                pltpu.VMEM((ob, rank, bs), BF16),
                pltpu.VMEM((2, 3, h * bs), F32),
                pltpu.VMEM((2, 1, h * bs), F32),
                pltpu.VMEM((2, ob, slots), jnp.int32),
                pltpu.VMEM((np_, window * bs), BF16),
                pltpu.VMEM((ROWS, own), F32),
                pltpu.VMEM((window, ROWS, bs), F32),
                pltpu.VMEM((ob, ROWS, bs), F32),
                pltpu.VMEM((ob, bs, 8 * ROWS), BF16),
                pltpu.VMEM((window, 8 * ROWS, bs), BF16),
                pltpu.VMEM(((2 * HALO + 1) * window + 1, 1, bs), F32),
                pltpu.VMEM((window, np_, bs), F32),
                pltpu.VMEM((ob, np_, bs), F32),
                pltpu.VMEM((n // 2, ob * rank // 2, 2 * np_), BF16),
                pltpu.VMEM((n // 2, ob, 128), F32),
                pltpu.VMEM((ob, 128), F32),
                pltpu.VMEM((ob * rank // 2, 2 * np_), F32),
                pltpu.VMEM((ob * rank // 2, 2 * np_), F32),
                pltpu.VMEM((2, bs, bs), BF16),
                dma((6,)), dma((2, 4)), dma((2, 4)), dma((ob,)), dma((ob,)),
                dma((n // 4,)), dma((n // 4,)), dma((n // 4,)), dma((n // 4,)), dma((4,)), dma((4,)),
            ],
            compiler_params=pltpu.CompilerParams(collective_id=0, has_side_effects=True, vmem_limit_bytes=60 * 1024 * 1024),
        )(coordinates, length_scale.reshape(1, own), probes, near_ids, basis_out, basis_in)

    placed = (
        P(None, ("grp", "row")),
        P(("grp", "row")),
        P(None, ("grp", "row")),
        P(("grp", "row"), None),
        P(("grp", "row")),
        P(("grp", "row"), None, None),
        P(("grp", "row"), None, None),
    )
    return jax.shard_map(
        shards, mesh=mesh, in_specs=placed, out_specs=P(None, ("grp", "row")), check_vma=False
    )
```

```python
import functools
import math

import jax
import jax.numpy as jnp
from jax import lax
from jax.experimental import pallas as pl
from jax.experimental.pallas import tpu as pltpu
from jax.sharding import PartitionSpec as P

HALO = 8
ROWS = 16
OPEN_AT = 1
LEVEL_AT = 6
SUM_AT = 7
BEFORE = 2
STRIP = 16
LOG2E = 1.0 / math.log(2.0)
C_SCALE = math.log(2.0) ** (-2.0 / 3.0)
D_SCALE = 3.0 * LOG2E * LOG2E * C_SCALE
F32 = jnp.float32
BF16 = jnp.bfloat16


def split3(x):
    high = x.astype(BF16)
    rest = x - high.astype(F32)
    mid = rest.astype(BF16)
    low = (rest - mid.astype(F32)).astype(BF16)
    return high, mid, low


def left_stack(x):
    h, m, l = [part.astype(F32) for part in split3(x)]
    return jnp.concatenate([h, h, m, h, l, m, m, l], axis=0)


def right_stack(x):
    h, m, l = split3(x)
    return jnp.concatenate([h, m, h, l, h, m, l, m], axis=0)


def matern(first, second):
    sq_dist = (first[0] - second[0]) * (first[0] - second[0])
    sq_dist = sq_dist + (first[1] - second[1]) * (first[1] - second[1])
    sq_dist = sq_dist + (first[2] - second[2]) * (first[2] - second[2])
    mean_sq = 0.5 * (first[3] * first[3] + second[3] * second[3])
    ratio = first[3] * second[3] / mean_sq
    prefac = ratio * jnp.sqrt(ratio)
    scaled = jnp.sqrt(3.0 * (sq_dist / mean_sq))
    return prefac * (1.0 + scaled) * jnp.exp(-scaled)


def nt(a, b):
    return lax.dot_general(a, b, (((1,), (1,)), ((), ())), preferred_element_type=F32)


def tn(a, b):
    return lax.dot_general(a, b, (((0,), (0,)), ((), ())), preferred_element_type=F32)


def nn(a, b):
    return lax.dot_general(a, b, (((1,), (0,)), ((), ())), preferred_element_type=F32)


def kernel(
    n, ob, bs,
    xyz_in, len_in, probes_in, ids_in, bout_in, bin_in, out_ref,
    xyz_ref, len_ref, ids_ref, bout_ref, bin_ref,
    xyz_h, len_h, ids_h, probes,
    rec_i, rec_j, cen_j, lhs, rhs_c, mask, acc, part,
    fold_all, cen_all, cen_y, own_sum, red_out, red_in,
    both, value_buf, load_sem, halo_send, halo_recv, part_send, part_recv,
    gat_send, gat_recv, cen_send, cen_recv, low_send, low_recv,
):
    me = lax.axis_index("row")
    own = ob * bs
    h = ob // 2
    window = ob + 2 * h
    hb = h * bs
    quads = n // 4
    core = me % 2
    col_y = me // 2 % 2
    hi = me // 4
    fast = me + 1 - 2 * core
    slow = jnp.clip(me - 1 + 2 * core, 0, n - 1)
    has_left = me > 0
    has_right = me < n - 1
    has_slow = jnp.where(core == 0, has_left, has_right)
    across = me + 2 - 4 * col_y
    side_fast = 1 - core
    side_slow = core
    half = bin_ref.shape[1] // 2
    np_ = probes.shape[0]
    width = n // 2 * ob

    loads = [
        pltpu.make_async_copy(src, dst, load_sem.at[k])
        for k, (src, dst) in enumerate(
            (
                (xyz_in, xyz_ref), (len_in, len_ref), (ids_in, ids_ref),
                (probes_in, probes.at[:, hb : hb + own]), (bin_in, bin_ref), (bout_in, bout_ref),
            )
        )
    ]
    for load in loads:
        load.start()

    barrier = pltpu.get_barrier_semaphore()

    def greet(peer):
        pl.semaphore_signal(barrier, inc=1, device_id={"row": peer})

    greet(fast)
    pl.when(has_slow)(lambda: greet(slow))
    greet(across)

    def level(k):
        return lax.rem(hi + k, quads) * 4 + me % 4

    for k in range(1, quads):
        greet(level(k))

    def lanes(start, size):
        return pl.ds(pl.multiple_of(start, size), size)

    def halo_out(side, peer):
        src = lanes(side * hb, hb)
        there = 1 - side
        pairs = (
            (xyz_in.at[:, src], xyz_h.at[there]),
            (len_in.at[:, src], len_h.at[there]),
            (ids_in, ids_h.at[there]),
            (probes_in.at[:, src], probes.at[:, lanes(there * (own + hb), hb)]),
        )
        return [
            pltpu.make_async_remote_copy(
                src_ref=a, dst_ref=b, send_sem=halo_send.at[side, k], recv_sem=halo_recv.at[there, k],
                device_id={"row": peer},
            )
            for k, (a, b) in enumerate(pairs)
        ]

    def halo_arrival(side, peer):
        pairs = (
            (xyz_in.at[:, 0:hb], xyz_h.at[side]),
            (len_in.at[:, 0:hb], len_h.at[side]),
            (ids_in, ids_h.at[side]),
            (probes_in.at[:, 0:hb], probes.at[:, lanes(side * (own + hb), hb)]),
        )
        return [
            pltpu.make_async_remote_copy(
                src_ref=a, dst_ref=b, send_sem=halo_send.at[side, k], recv_sem=halo_recv.at[side, k],
                device_id={"row": peer},
            )
            for k, (a, b) in enumerate(pairs)
        ]

    slot = core * quads + hi

    def level_copies(k, source):
        at = core * quads + source
        return [
            pltpu.make_async_remote_copy(
                src_ref=fold_all.at[at], dst_ref=fold_all.at[at],
                send_sem=gat_send.at[k], recv_sem=gat_recv.at[k], device_id={"row": level(k)},
            ),
            pltpu.make_async_remote_copy(
                src_ref=cen_all.at[at], dst_ref=cen_all.at[at],
                send_sem=cen_send.at[k], recv_sem=cen_recv.at[k], device_id={"row": level(k)},
            ),
        ]

    def core_copies(which):
        held = pl.ds(which * quads, quads)
        return [
            pltpu.make_async_remote_copy(
                src_ref=fold_all.at[held], dst_ref=fold_all.at[held],
                send_sem=low_send.at[0], recv_sem=low_recv.at[0], device_id={"row": fast},
            ),
            pltpu.make_async_remote_copy(
                src_ref=cen_all.at[held], dst_ref=cen_all.at[held],
                send_sem=low_send.at[1], recv_sem=low_recv.at[1], device_id={"row": fast},
            ),
        ]

    center_copy = pltpu.make_async_remote_copy(
        src_ref=cen_all.at[slot], dst_ref=cen_y,
        send_sem=low_send.at[2], recv_sem=low_recv.at[2], device_id={"row": across},
    )
    sum_copy = pltpu.make_async_remote_copy(
        src_ref=red_out, dst_ref=red_in,
        send_sem=low_send.at[3], recv_sem=low_recv.at[3], device_id={"row": across},
    )

    def part_copy(side, x, peer):
        return pltpu.make_async_remote_copy(
            src_ref=acc.at[(ob + h) * side + x], dst_ref=part.at[h * (1 - side) + x],
            send_sem=part_send.at[side * h + x], recv_sem=part_recv.at[h * (1 - side) + x],
            device_id={"row": peer},
        )

    def part_arrival(b, peer):
        return pltpu.make_async_remote_copy(
            src_ref=acc.at[b], dst_ref=part.at[b],
            send_sem=part_send.at[b], recv_sem=part_recv.at[b], device_id={"row": peer},
        )

    for load in loads[:5]:
        load.wait()
    row = lax.broadcasted_iota(jnp.int32, (ROWS, bs), 0)

    def fill_j(at, xyz, ln):
        rec_j[at, 0:3, :] = xyz
        rec_j[at, 3:6, :] = jnp.ones((3, bs), F32)
        rec_j[at, 6:9, :] = xyz
        rec_j[at, 9:10, :] = jnp.ones((1, bs), F32)
        rec_j[at, 10:11, :] = ln * ln
        rec_j[at, 11:12, :] = 1.0 / ln
        rec_j[at, 12:16, :] = jnp.zeros((4, bs), F32)
        feat = jnp.where((row == 9) | (row == 10), rec_j[at], 0.0) * (rec_j[at, 11:12, :] * (0.5 * C_SCALE))
        rhs_c[at] = right_stack(feat)

    rec_i[0:3, :] = xyz_ref[...]
    rec_i[3:6, :] = xyz_ref[...]
    rec_i[6:9, :] = jnp.ones((3, own), F32)
    ln0 = len_ref[...]
    rec_i[9:10, :] = ln0 * ln0
    rec_i[10:11, :] = jnp.ones((1, own), F32)
    rec_i[11:12, :] = ln0
    rec_i[12:16, :] = jnp.zeros((4, own), F32)

    ids = ids_ref[...]
    slots = ids.shape[1]
    lane = lax.broadcasted_iota(jnp.int32, (ROWS, 128), 1)
    own_centers = jnp.zeros((ROWS, 128), F32)
    for b in range(ob):
        blk = rec_i[:, b * bs : (b + 1) * bs]
        mean = jnp.sum(blk, axis=1, keepdims=True) * (1.0 / bs)
        own_centers = jnp.where(lane == b, mean, own_centers)
        mean_w = jnp.broadcast_to(mean, (ROWS, bs))
        cen = jnp.where(row < 6, mean_w, 0.0)
        v = blk - cen
        feat = jnp.where((row >= 3) & (row < 6), v * v, jnp.where(row < 11, v, 0.0)) * (1.0 / rec_i[11:12, b * bs : (b + 1) * bs])
        lhs[b] = left_stack(feat).T.astype(BF16)
        fill_j(h + b, xyz_ref[:, b * bs : (b + 1) * bs], len_ref[:, b * bs : (b + 1) * bs])
        mean_j = jnp.sum(rec_j[h + b], axis=1, keepdims=True) * (1.0 / bs)
        cen_j[b] = jnp.where((row < 3) | ((row >= 6) & (row < 9)), jnp.broadcast_to(mean_j, (ROWS, bs)), 0.0)
        pb = probes[:, hb + b * bs : hb + (b + 1) * bs]
        fold = jnp.concatenate([nt(bin_ref[b, 0:half, :], pb), nt(bin_ref[b, half:, :], pb)], axis=1)
        fold_all[slot, b * half : (b + 1) * half, :] = fold.astype(BF16)
    square = jnp.concatenate([own_centers, jnp.zeros((128 - ROWS, 128), F32)], axis=0).T
    id_rows = jnp.concatenate(
        [jnp.zeros((ob, ROWS), F32), ids.astype(F32), jnp.zeros((ob, 128 - ROWS - slots), F32)], axis=1
    )
    own_cols = square[0:ob, :] + id_rows
    cen_all[slot] = own_cols

    acc[...] = jnp.zeros_like(acc)

    def member(ids, target):
        return jnp.max(jnp.where(ids == target, 1.0, 0.0), axis=1, keepdims=True)

    gid = lax.broadcasted_iota(jnp.int32, ids.shape, 0) + me * ob

    def mask_at(offset, q):
        return (offset + HALO) * window + q

    for offset in range(-HALO, HALO + 1):
        wide = jnp.broadcast_to(member(ids, gid + offset), (ob, bs))
        for b in range(ob):
            mask[mask_at(offset, h + b)] = wide[b : b + 1, :]
    blank = (2 * HALO + 1) * window
    mask[blank] = jnp.zeros((1, bs), F32)

    def right_side(o, q):
        v = rec_j[q] - cen_j[o]
        feat = jnp.where(
            row < 3, (-2.0 * D_SCALE) * v,
            jnp.where(row < 6, D_SCALE, jnp.where(row < 9, D_SCALE * v * v, 0.0)),
        ) * rec_j[q, 11:12, :]
        return jnp.concatenate([right_stack(feat), rhs_c[q]], axis=1)

    def entries(o, q, turn):
        both[turn] = nn(lhs[o], right_side(o, q))

    def values(turn):
        for r in range(0, bs, STRIP):
            e = jnp.maximum(both[turn, r : r + STRIP, :bs], 1e-30)
            q = both[turn, r : r + STRIP, bs:]
            s = e * lax.rsqrt(e * q)
            value_buf[turn, r : r + STRIP, :] = ((LOG2E + s) * jnp.exp2(-1.5 * lax.log2(q) - s)).astype(BF16)

    def products(o, q, turn):
        offset = q - h - o
        value = value_buf[turn]
        p_q = probes[:, lanes(q * bs, bs)]
        p_o = probes[:, lanes((h + o) * bs, bs)]
        acc[h + o] += mask[mask_at(offset, h + o)] * nt(p_q, value)
        acc[q] += mask[jnp.where(offset == 0, blank, mask_at(-offset, q))] * nn(p_o, value)

    def sweep(pairs):
        entries(*pairs[0], 0)
        for t, pair in enumerate(pairs):
            if t + 1 < len(pairs):
                entries(*pairs[t + 1], (t + 1) % 2)
            values(t % 2)
            if t:
                products(*pairs[t - 1], (t - 1) % 2)
        products(*pairs[-1], (len(pairs) - 1) % 2)

    table = []
    for g in range(h):
        c = [(s + g) // ob for s in range(ob + 1)]
        first = [g + k * (ob - 1 - 2 * g) for k in c]
        table.append([(f, h + f + s - k * (ob - g)) for s, (k, f) in enumerate(zip(c, first))])
    for g in range(h // 2):
        cols = [(g, ob), (h - 1 - g, h)]
        table.append([(i, h + ob + c) for c, stop in cols for i in range(c, stop)])
    for g in range(h // 2):
        table.append([(c, i - h) for i in (h + g, ob - 1 - g) for c in range(h // 2, i + 1)])

    def pick(kind, entries):
        out = jnp.int32(entries[0])
        for k in range(1, len(entries)):
            if entries[k] != entries[0]:
                out = jnp.where(kind == k, entries[k], out)
        return out

    def open_links():
        pl.semaphore_wait(barrier, quads + 1 + jnp.where(has_slow, 1, 0))

        @pl.when(has_slow)
        def _():
            for copy in halo_out(side_slow, slow):
                copy.start()

        for copy in halo_out(side_fast, fast):
            copy.start()
        for k in range(1, quads):
            for copy in level_copies(k, hi):
                copy.start()
        center_copy.start()

    def take_halo(side):
        first = side * (ob + h)
        for b in range(h):
            fill_j(first + b, xyz_h[side, :, b * bs : (b + 1) * bs], len_h[side, :, b * bs : (b + 1) * bs])
        there = ids_h[side]
        sign = 1 - 2 * side
        base = gid + (2 * side - 1) * ob
        for dj in range(1, HALO + 1):
            wide = jnp.broadcast_to(member(there, base + sign * dj), (ob, bs))
            part_rows = jnp.where(side == 0, wide[h:, :], wide[:h, :])
            for b in range(h):
                mask[mask_at(sign * dj, first + b)] = part_rows[b : b + 1, :]

    def take_fast():
        for copy in halo_arrival(side_fast, fast):
            copy.wait_recv()
        take_halo(side_fast)

    def take_slow():
        @pl.when(has_slow)
        def _():
            for copy in halo_arrival(side_slow, slow):
                copy.wait_recv()

        @pl.when(jnp.logical_not(has_slow))
        def _():
            xyz_h[side_slow] = xyz_ref[:, 0:hb]
            len_h[side_slow] = len_ref[:, 0:hb]
            ids_h[side_slow] = ids_ref[...]
            probes[:, lanes(side_slow * (own + hb), hb)] = probes[:, hb : 2 * hb]

        take_halo(side_slow)

    def level_done():
        for k in range(1, quads):
            for copy in level_copies(k, hi):
                copy.wait()
        for copy in core_copies(core):
            copy.start()

    step_w = min(128, width)

    def partial_sums():
        for copy in core_copies(core):
            copy.wait()
        center_copy.wait()
        centers = cen_all[...].reshape(width, 128).T
        mine = cen_all[slot]
        column = lax.broadcasted_iota(jnp.int32, (ob, width), 1)
        holder = column // ob
        device = holder % quads * 4 + col_y * 2 + holder // quads
        global_ids = (device * ob + column % ob).astype(F32)
        picks = (0, 1, 2, 11)
        pick_r = lax.broadcasted_iota(jnp.int32, (step_w, step_w * half), 0)
        pick_c = lax.broadcasted_iota(jnp.int32, (step_w, step_w * half), 1)
        spread = jnp.where(pick_c // half == pick_r, 1.0, 0.0).astype(BF16)
        eye_r = lax.broadcasted_iota(jnp.int32, (ob * half, step_w * half), 0)
        eye_c = lax.broadcasted_iota(jnp.int32, (ob * half, step_w * half), 1)
        same = lax.rem(eye_r, half) == lax.rem(eye_c, half)
        per = step_w // ob
        totals = []
        for rows in (mine, cen_y[...]):
            coupling = matern([rows[:, c : c + 1] for c in picks], [centers[c : c + 1, :] for c in picks])
            near = jnp.zeros((ob, width), F32)
            for t in range(slots):
                near = jnp.where(rows[:, ROWS + t : ROWS + t + 1] == global_ids, 1.0, near)
            coupling = jnp.where(near > 0.0, 0.0, coupling).astype(BF16)
            total = jnp.zeros((ob * half, 2 * np_), F32)
            for q in range(width // step_w):
                wide = nn(coupling[:, q * step_w : (q + 1) * step_w], spread)
                wide = jnp.concatenate(
                    [jnp.broadcast_to(wide[i : i + 1, :], (half, step_w * half)) for i in range(ob)], axis=0
                )
                kron = jnp.where(same, wide, 0.0).astype(BF16)
                folded = fold_all[q * per : (q + 1) * per].reshape(step_w * half, 2 * np_)
                total = total + nn(kron, folded)
            totals.append(total)
        red_out[...] = totals[1]
        own_sum[...] = totals[0]
        sum_copy.start()

    before = min(BEFORE, h)
    hooks = [(OPEN_AT, open_links), (before, take_fast), (before + h // 2, take_slow)]
    hooks += [(LEVEL_AT, level_done), (SUM_AT, partial_sums)]

    def group(t, carry):
        for at, hook in hooks:
            if at < ob:
                pl.when(t == at)(hook)
        crossing = jnp.logical_and(t >= before, t < before + h)
        swapped = h + (t - before + core * (h // 2) + h) % h
        kind = jnp.where(crossing, swapped, jnp.where(t < before, t, t - h))
        sweep(
            [
                (pick(kind, [tiles[s][0] for tiles in table]), pick(kind, [tiles[s][1] for tiles in table]))
                for s in range(ob + 1)
            ]
        )
        g = (kind - h + h) % (h // 2)
        side = jnp.where(kind < h + h // 2, 1, 0)
        is_fast = t < before + h // 2
        peer = jnp.where(is_fast, fast, slow)

        @pl.when(jnp.logical_and(crossing, jnp.logical_or(is_fast, has_slow)))
        def _():
            part_copy(side, g, peer).start()
            part_copy(side, h - 1 - g, peer).start()

        return carry

    lax.fori_loop(0, ob, group, 0)

    for at, hook in hooks:
        if at >= ob:
            hook()
    loads[5].wait()

    for x in range(h):
        part_arrival(side_fast * h + x, fast).wait_recv()

    @pl.when(has_slow)
    def _():
        for x in range(h):
            part_arrival(side_slow * h + x, slow).wait_recv()

    @pl.when(jnp.logical_not(has_slow))
    def _():
        for x in range(h):
            part[side_slow * h + x] = jnp.zeros((np_, bs), F32)

    sum_copy.wait()
    summed = (own_sum[...] + red_in[...]).astype(BF16)
    for b in range(ob):
        mine = summed[b * half : (b + 1) * half, :]
        far = tn(mine[:, :np_], bout_ref[b, 0:half, :]) + tn(mine[:, np_:], bout_ref[b, half:, :])
        out_ref[:, b * bs : (b + 1) * bs] = acc[h + b] + part[b] + far

    for copy in halo_out(side_fast, fast):
        copy.wait_send()
    for x in range(h):
        part_copy(side_fast, x, fast).wait_send()

    @pl.when(has_slow)
    def _():
        for copy in halo_out(side_slow, slow):
            copy.wait_send()
        for x in range(h):
            part_copy(side_slow, x, slow).wait_send()


def solution(mesh):
    n = mesh.shape["row"]

    def shards(coordinates, length_scale, probes, near_ids, near_count, basis_out, basis_in):
        ob, rank, bs = basis_out.shape
        np_ = probes.shape[0]
        own = ob * bs
        h = ob // 2
        slots = near_ids.shape[1]
        window = ob + 2 * h
        vmem = pl.BlockSpec(memory_space=pltpu.VMEM)
        dma = pltpu.SemaphoreType.DMA
        return pl.pallas_call(
            functools.partial(kernel, n, ob, bs),
            out_shape=jax.ShapeDtypeStruct((np_, own), F32),
            in_specs=[pl.BlockSpec(memory_space=pl.ANY)] * 6,
            out_specs=vmem,
            scratch_shapes=[
                pltpu.VMEM((3, own), F32),
                pltpu.VMEM((1, own), F32),
                pltpu.VMEM((ob, slots), jnp.int32),
                pltpu.VMEM((ob, rank, bs), BF16),
                pltpu.VMEM((ob, rank, bs), BF16),
                pltpu.VMEM((2, 3, h * bs), F32),
                pltpu.VMEM((2, 1, h * bs), F32),
                pltpu.VMEM((2, ob, slots), jnp.int32),
                pltpu.VMEM((np_, window * bs), BF16),
                pltpu.VMEM((ROWS, own), F32),
                pltpu.VMEM((window, ROWS, bs), F32),
                pltpu.VMEM((ob, ROWS, bs), F32),
                pltpu.VMEM((ob, bs, 8 * ROWS), BF16),
                pltpu.VMEM((window, 8 * ROWS, bs), BF16),
                pltpu.VMEM(((2 * HALO + 1) * window + 1, 1, bs), F32),
                pltpu.VMEM((window, np_, bs), F32),
                pltpu.VMEM((ob, np_, bs), F32),
                pltpu.VMEM((n // 2, ob * rank // 2, 2 * np_), BF16),
                pltpu.VMEM((n // 2, ob, 128), F32),
                pltpu.VMEM((ob, 128), F32),
                pltpu.VMEM((ob * rank // 2, 2 * np_), F32),
                pltpu.VMEM((ob * rank // 2, 2 * np_), F32),
                pltpu.VMEM((ob * rank // 2, 2 * np_), F32),
                pltpu.VMEM((2, bs, 2 * bs), F32),
                pltpu.VMEM((2, bs, bs), BF16),
                dma((6,)), dma((2, 4)), dma((2, 4)), dma((ob,)), dma((ob,)),
                dma((n // 4,)), dma((n // 4,)), dma((n // 4,)), dma((n // 4,)), dma((4,)), dma((4,)),
            ],
            compiler_params=pltpu.CompilerParams(collective_id=0, has_side_effects=True, vmem_limit_bytes=60 * 1024 * 1024),
        )(coordinates, length_scale.reshape(1, own), probes, near_ids, basis_out, basis_in)

    placed = (
        P(None, ("grp", "row")),
        P(("grp", "row")),
        P(None, ("grp", "row")),
        P(("grp", "row"), None),
        P(("grp", "row")),
        P(("grp", "row"), None, None),
        P(("grp", "row"), None, None),
    )
    return jax.shard_map(
        shards, mesh=mesh, in_specs=placed, out_specs=P(None, ("grp", "row")), check_vma=False
    )
```

```python
import functools
import math

import jax
import jax.numpy as jnp
from jax import lax
from jax.experimental import pallas as pl
from jax.experimental.pallas import tpu as pltpu
from jax.sharding import PartitionSpec as P

HALO = 8
ROWS = 16
OPEN_AT = 1
LEVEL_AT = 6
SUM_AT = 7
BEFORE = 2
STRIP = 16
LOG2E = 1.0 / math.log(2.0)
C_SCALE = math.log(2.0) ** (-2.0 / 3.0)
D_SCALE = 3.0 * LOG2E * LOG2E * C_SCALE
F32 = jnp.float32
BF16 = jnp.bfloat16


def split3(x):
    high = x.astype(BF16)
    rest = x - high.astype(F32)
    mid = rest.astype(BF16)
    low = (rest - mid.astype(F32)).astype(BF16)
    return high, mid, low


def left_stack(x):
    h, m, l = [part.astype(F32) for part in split3(x)]
    return jnp.concatenate([h, h, m, h, l, m, m, l], axis=0)


def right_stack(x):
    h, m, l = split3(x)
    return jnp.concatenate([h, m, h, l, h, m, l, m], axis=0)


def matern(first, second):
    sq_dist = (first[0] - second[0]) * (first[0] - second[0])
    sq_dist = sq_dist + (first[1] - second[1]) * (first[1] - second[1])
    sq_dist = sq_dist + (first[2] - second[2]) * (first[2] - second[2])
    mean_sq = 0.5 * (first[3] * first[3] + second[3] * second[3])
    ratio = first[3] * second[3] / mean_sq
    prefac = ratio * jnp.sqrt(ratio)
    scaled = jnp.sqrt(3.0 * (sq_dist / mean_sq))
    return prefac * (1.0 + scaled) * jnp.exp(-scaled)


def nt(a, b):
    return lax.dot_general(a, b, (((1,), (1,)), ((), ())), preferred_element_type=F32)


def tn(a, b):
    return lax.dot_general(a, b, (((0,), (0,)), ((), ())), preferred_element_type=F32)


def nn(a, b):
    return lax.dot_general(a, b, (((1,), (0,)), ((), ())), preferred_element_type=F32)


def kernel(
    n, ob, bs,
    xyz_in, len_in, probes_in, ids_in, bout_in, bin_in, out_ref,
    xyz_ref, len_ref, ids_ref, bout_ref, bin_ref,
    xyz_h, len_h, ids_h, probes,
    rec_i, rec_j, cen_j, lhs, rhs_c, mask, acc, part,
    fold_all, cen_all, cen_y, own_sum, red_out, red_in,
    both, value_buf, load_sem, halo_send, halo_recv, part_send, part_recv,
    gat_send, gat_recv, cen_send, cen_recv, low_send, low_recv,
):
    me = lax.axis_index("row")
    own = ob * bs
    h = ob // 2
    window = ob + 2 * h
    hb = h * bs
    quads = n // 4
    core = me % 2
    col_y = me // 2 % 2
    hi = me // 4
    fast = me + 1 - 2 * core
    slow = jnp.clip(me - 1 + 2 * core, 0, n - 1)
    has_left = me > 0
    has_right = me < n - 1
    has_slow = jnp.where(core == 0, has_left, has_right)
    across = me + 2 - 4 * col_y
    side_fast = 1 - core
    side_slow = core
    half = bin_ref.shape[1] // 2
    np_ = probes.shape[0]
    width = n // 2 * ob

    loads = [
        pltpu.make_async_copy(src, dst, load_sem.at[k])
        for k, (src, dst) in enumerate(
            (
                (xyz_in, xyz_ref), (len_in, len_ref), (ids_in, ids_ref),
                (probes_in, probes.at[:, hb : hb + own]), (bin_in, bin_ref), (bout_in, bout_ref),
            )
        )
    ]
    for load in loads:
        load.start()

    barrier = pltpu.get_barrier_semaphore()

    def greet(peer):
        pl.semaphore_signal(barrier, inc=1, device_id={"row": peer})

    greet(fast)
    pl.when(has_slow)(lambda: greet(slow))
    greet(across)

    def level(k):
        return lax.rem(hi + k, quads) * 4 + me % 4

    for k in range(1, quads):
        greet(level(k))

    def lanes(start, size):
        return pl.ds(pl.multiple_of(start, size), size)

    def halo_out(side, peer):
        src = lanes(side * hb, hb)
        there = 1 - side
        pairs = (
            (xyz_in.at[:, src], xyz_h.at[there]),
            (len_in.at[:, src], len_h.at[there]),
            (ids_in, ids_h.at[there]),
            (probes_in.at[:, src], probes.at[:, lanes(there * (own + hb), hb)]),
        )
        return [
            pltpu.make_async_remote_copy(
                src_ref=a, dst_ref=b, send_sem=halo_send.at[side, k], recv_sem=halo_recv.at[there, k],
                device_id={"row": peer},
            )
            for k, (a, b) in enumerate(pairs)
        ]

    def halo_arrival(side, peer):
        pairs = (
            (xyz_in.at[:, 0:hb], xyz_h.at[side]),
            (len_in.at[:, 0:hb], len_h.at[side]),
            (ids_in, ids_h.at[side]),
            (probes_in.at[:, 0:hb], probes.at[:, lanes(side * (own + hb), hb)]),
        )
        return [
            pltpu.make_async_remote_copy(
                src_ref=a, dst_ref=b, send_sem=halo_send.at[side, k], recv_sem=halo_recv.at[side, k],
                device_id={"row": peer},
            )
            for k, (a, b) in enumerate(pairs)
        ]

    slot = core * quads + hi

    def level_copies(k, source):
        at = core * quads + source
        return [
            pltpu.make_async_remote_copy(
                src_ref=fold_all.at[at], dst_ref=fold_all.at[at],
                send_sem=gat_send.at[k], recv_sem=gat_recv.at[k], device_id={"row": level(k)},
            ),
            pltpu.make_async_remote_copy(
                src_ref=cen_all.at[at], dst_ref=cen_all.at[at],
                send_sem=cen_send.at[k], recv_sem=cen_recv.at[k], device_id={"row": level(k)},
            ),
        ]

    def core_copies(which):
        held = pl.ds(which * quads, quads)
        return [
            pltpu.make_async_remote_copy(
                src_ref=fold_all.at[held], dst_ref=fold_all.at[held],
                send_sem=low_send.at[0], recv_sem=low_recv.at[0], device_id={"row": fast},
            ),
            pltpu.make_async_remote_copy(
                src_ref=cen_all.at[held], dst_ref=cen_all.at[held],
                send_sem=low_send.at[1], recv_sem=low_recv.at[1], device_id={"row": fast},
            ),
        ]

    center_copy = pltpu.make_async_remote_copy(
        src_ref=cen_all.at[slot], dst_ref=cen_y,
        send_sem=low_send.at[2], recv_sem=low_recv.at[2], device_id={"row": across},
    )
    sum_copy = pltpu.make_async_remote_copy(
        src_ref=red_out, dst_ref=red_in,
        send_sem=low_send.at[3], recv_sem=low_recv.at[3], device_id={"row": across},
    )

    def part_copy(side, x, peer):
        return pltpu.make_async_remote_copy(
            src_ref=acc.at[(ob + h) * side + x], dst_ref=part.at[h * (1 - side) + x],
            send_sem=part_send.at[side * h + x], recv_sem=part_recv.at[h * (1 - side) + x],
            device_id={"row": peer},
        )

    def part_arrival(b, peer):
        return pltpu.make_async_remote_copy(
            src_ref=acc.at[b], dst_ref=part.at[b],
            send_sem=part_send.at[b], recv_sem=part_recv.at[b], device_id={"row": peer},
        )

    for load in loads[:5]:
        load.wait()
    row = lax.broadcasted_iota(jnp.int32, (ROWS, bs), 0)

    def fill_j(at, xyz, ln):
        rec_j[at, 0:3, :] = xyz
        rec_j[at, 3:6, :] = jnp.ones((3, bs), F32)
        rec_j[at, 6:9, :] = xyz
        rec_j[at, 9:10, :] = jnp.ones((1, bs), F32)
        rec_j[at, 10:11, :] = ln * ln
        rec_j[at, 11:12, :] = 1.0 / ln
        rec_j[at, 12:16, :] = jnp.zeros((4, bs), F32)
        feat = jnp.where((row == 9) | (row == 10), rec_j[at], 0.0) * (rec_j[at, 11:12, :] * (0.5 * C_SCALE))
        rhs_c[at] = right_stack(feat)

    rec_i[0:3, :] = xyz_ref[...]
    rec_i[3:6, :] = xyz_ref[...]
    rec_i[6:9, :] = jnp.ones((3, own), F32)
    ln0 = len_ref[...]
    rec_i[9:10, :] = ln0 * ln0
    rec_i[10:11, :] = jnp.ones((1, own), F32)
    rec_i[11:12, :] = ln0
    rec_i[12:16, :] = jnp.zeros((4, own), F32)

    ids = ids_ref[...]
    slots = ids.shape[1]
    lane = lax.broadcasted_iota(jnp.int32, (ROWS, 128), 1)
    own_centers = jnp.zeros((ROWS, 128), F32)
    for b in range(ob):
        blk = rec_i[:, b * bs : (b + 1) * bs]
        mean = jnp.sum(blk, axis=1, keepdims=True) * (1.0 / bs)
        own_centers = jnp.where(lane == b, mean, own_centers)
        mean_w = jnp.broadcast_to(mean, (ROWS, bs))
        cen = jnp.where(row < 6, mean_w, 0.0)
        v = blk - cen
        feat = jnp.where((row >= 3) & (row < 6), v * v, jnp.where(row < 11, v, 0.0)) * (1.0 / rec_i[11:12, b * bs : (b + 1) * bs])
        lhs[b] = left_stack(feat).T.astype(BF16)
        fill_j(h + b, xyz_ref[:, b * bs : (b + 1) * bs], len_ref[:, b * bs : (b + 1) * bs])
        mean_j = jnp.sum(rec_j[h + b], axis=1, keepdims=True) * (1.0 / bs)
        cen_j[b] = jnp.where((row < 3) | ((row >= 6) & (row < 9)), jnp.broadcast_to(mean_j, (ROWS, bs)), 0.0)
        pb = probes[:, hb + b * bs : hb + (b + 1) * bs]
        fold = jnp.concatenate([nt(bin_ref[b, 0:half, :], pb), nt(bin_ref[b, half:, :], pb)], axis=1)
        fold_all[slot, b * half : (b + 1) * half, :] = fold.astype(BF16)
    square = jnp.concatenate([own_centers, jnp.zeros((128 - ROWS, 128), F32)], axis=0).T
    id_rows = jnp.concatenate(
        [jnp.zeros((ob, ROWS), F32), ids.astype(F32), jnp.zeros((ob, 128 - ROWS - slots), F32)], axis=1
    )
    own_cols = square[0:ob, :] + id_rows
    cen_all[slot] = own_cols

    acc[...] = jnp.zeros_like(acc)

    def member(ids, target):
        return jnp.max(jnp.where(ids == target, 1.0, 0.0), axis=1, keepdims=True)

    gid = lax.broadcasted_iota(jnp.int32, ids.shape, 0) + me * ob

    def mask_at(offset, q):
        return (offset + HALO) * window + q

    for offset in range(-HALO, HALO + 1):
        wide = jnp.broadcast_to(member(ids, gid + offset), (ob, bs))
        for b in range(ob):
            mask[mask_at(offset, h + b)] = wide[b : b + 1, :]
    blank = (2 * HALO + 1) * window
    mask[blank] = jnp.zeros((1, bs), F32)

    def right_side(o, q):
        v = rec_j[q] - cen_j[o]
        feat = jnp.where(
            row < 3, (-2.0 * D_SCALE) * v,
            jnp.where(row < 6, D_SCALE, jnp.where(row < 9, D_SCALE * v * v, 0.0)),
        ) * rec_j[q, 11:12, :]
        return jnp.concatenate([right_stack(feat), rhs_c[q]], axis=1)

    def entries(o, q, turn):
        both[turn] = nn(lhs[o], right_side(o, q))

    def values(turn):
        for r in range(0, bs, STRIP):
            e = jnp.maximum(both[turn, r : r + STRIP, :bs], 1e-30)
            q = both[turn, r : r + STRIP, bs:]
            s = e * lax.rsqrt(e * q)
            value_buf[turn, r : r + STRIP, :] = ((LOG2E + s) * jnp.exp2(-1.5 * lax.log2(q) - s)).astype(BF16)

    def products(o, q, turn):
        offset = q - h - o
        value = value_buf[turn]
        p_q = probes[:, lanes(q * bs, bs)]
        p_o = probes[:, lanes((h + o) * bs, bs)]
        acc[h + o] += mask[mask_at(offset, h + o)] * nt(p_q, value)
        acc[q] += mask[jnp.where(offset == 0, blank, mask_at(-offset, q))] * nn(p_o, value)

    def sweep(pairs):
        entries(*pairs[0], 0)
        for t, pair in enumerate(pairs):
            if t + 1 < len(pairs):
                entries(*pairs[t + 1], (t + 1) % 2)
            values(t % 2)
            if t:
                products(*pairs[t - 1], (t - 1) % 2)
        products(*pairs[-1], (len(pairs) - 1) % 2)

    table = []
    for g in range(h):
        c = [(s + g) // ob for s in range(ob + 1)]
        first = [g + k * (ob - 1 - 2 * g) for k in c]
        table.append([(f, h + f + s - k * (ob - g)) for s, (k, f) in enumerate(zip(c, first))])
    for g in range(h // 2):
        cols = [(g, ob), (h - 1 - g, h)]
        table.append([(i, h + ob + c) for c, stop in cols for i in range(c, stop)])
    for g in range(h // 2):
        table.append([(c, i - h) for i in (h + g, ob - 1 - g) for c in range(h // 2, i + 1)])

    def pick(kind, entries):
        out = jnp.int32(entries[0])
        for k in range(1, len(entries)):
            if entries[k] != entries[0]:
                out = jnp.where(kind == k, entries[k], out)
        return out

    def open_links():
        pl.semaphore_wait(barrier, quads + 1 + jnp.where(has_slow, 1, 0))

        @pl.when(has_slow)
        def _():
            for copy in halo_out(side_slow, slow):
                copy.start()

        for copy in halo_out(side_fast, fast):
            copy.start()
        for k in range(1, quads):
            for copy in level_copies(k, hi):
                copy.start()
        center_copy.start()

    def take_halo(side):
        first = side * (ob + h)
        for b in range(h):
            fill_j(first + b, xyz_h[side, :, b * bs : (b + 1) * bs], len_h[side, :, b * bs : (b + 1) * bs])
        there = ids_h[side]
        sign = 1 - 2 * side
        base = gid + (2 * side - 1) * ob
        for dj in range(1, HALO + 1):
            wide = jnp.broadcast_to(member(there, base + sign * dj), (ob, bs))
            part_rows = jnp.where(side == 0, wide[h:, :], wide[:h, :])
            for b in range(h):
                mask[mask_at(sign * dj, first + b)] = part_rows[b : b + 1, :]

    def take_fast():
        for copy in halo_arrival(side_fast, fast):
            copy.wait_recv()
        take_halo(side_fast)

    def take_slow():
        @pl.when(has_slow)
        def _():
            for copy in halo_arrival(side_slow, slow):
                copy.wait_recv()

        @pl.when(jnp.logical_not(has_slow))
        def _():
            xyz_h[side_slow] = xyz_ref[:, 0:hb]
            len_h[side_slow] = len_ref[:, 0:hb]
            ids_h[side_slow] = ids_ref[...]
            probes[:, lanes(side_slow * (own + hb), hb)] = probes[:, hb : 2 * hb]

        take_halo(side_slow)

    def level_done():
        for k in range(1, quads):
            for copy in level_copies(k, hi):
                copy.wait()
        for copy in core_copies(core):
            copy.start()

    step_w = min(128, width)

    def partial_sums():
        for copy in core_copies(core):
            copy.wait()
        center_copy.wait()
        centers = cen_all[...].reshape(width, 128).T
        mine = cen_all[slot]
        column = lax.broadcasted_iota(jnp.int32, (ob, width), 1)
        holder = column // ob
        device = holder % quads * 4 + col_y * 2 + holder // quads
        global_ids = (device * ob + column % ob).astype(F32)
        picks = (0, 1, 2, 11)
        pick_r = lax.broadcasted_iota(jnp.int32, (step_w, step_w * half), 0)
        pick_c = lax.broadcasted_iota(jnp.int32, (step_w, step_w * half), 1)
        spread = jnp.where(pick_c // half == pick_r, 1.0, 0.0).astype(BF16)
        eye_r = lax.broadcasted_iota(jnp.int32, (ob * half, step_w * half), 0)
        eye_c = lax.broadcasted_iota(jnp.int32, (ob * half, step_w * half), 1)
        same = lax.rem(eye_r, half) == lax.rem(eye_c, half)
        per = step_w // ob
        totals = []
        for rows in (mine, cen_y[...]):
            coupling = matern([rows[:, c : c + 1] for c in picks], [centers[c : c + 1, :] for c in picks])
            near = jnp.zeros((ob, width), F32)
            for t in range(slots):
                near = jnp.where(rows[:, ROWS + t : ROWS + t + 1] == global_ids, 1.0, near)
            coupling = jnp.where(near > 0.0, 0.0, coupling).astype(BF16)
            total = jnp.zeros((ob * half, 2 * np_), F32)
            for q in range(width // step_w):
                wide = nn(coupling[:, q * step_w : (q + 1) * step_w], spread)
                wide = jnp.concatenate(
                    [jnp.broadcast_to(wide[i : i + 1, :], (half, step_w * half)) for i in range(ob)], axis=0
                )
                kron = jnp.where(same, wide, 0.0).astype(BF16)
                folded = fold_all[q * per : (q + 1) * per].reshape(step_w * half, 2 * np_)
                total = total + nn(kron, folded)
            totals.append(total)
        red_out[...] = totals[1]
        own_sum[...] = totals[0]
        sum_copy.start()

    before = min(BEFORE, h)
    hooks = [(OPEN_AT, open_links), (before, take_fast), (before + h // 2, take_slow)]
    hooks += [(LEVEL_AT, level_done), (SUM_AT, partial_sums)]

    def group(t, carry):
        for at, hook in hooks:
            if at < ob:
                pl.when(t == at)(hook)
        crossing = jnp.logical_and(t >= before, t < before + h)
        swapped = h + (t - before + core * (h // 2) + h) % h
        kind = jnp.where(crossing, swapped, jnp.where(t < before, t, t - h))
        sweep(
            [
                (pick(kind, [tiles[s][0] for tiles in table]), pick(kind, [tiles[s][1] for tiles in table]))
                for s in range(ob + 1)
            ]
        )
        g = (kind - h + h) % (h // 2)
        side = jnp.where(kind < h + h // 2, 1, 0)
        is_fast = t < before + h // 2
        peer = jnp.where(is_fast, fast, slow)

        @pl.when(jnp.logical_and(crossing, jnp.logical_or(is_fast, has_slow)))
        def _():
            part_copy(side, g, peer).start()
            part_copy(side, h - 1 - g, peer).start()

        return carry

    lax.fori_loop(0, ob, group, 0)

    for at, hook in hooks:
        if at >= ob:
            hook()
    loads[5].wait()

    for x in range(h):
        part_arrival(side_fast * h + x, fast).wait_recv()

    @pl.when(has_slow)
    def _():
        for x in range(h):
            part_arrival(side_slow * h + x, slow).wait_recv()

    @pl.when(jnp.logical_not(has_slow))
    def _():
        for x in range(h):
            part[side_slow * h + x] = jnp.zeros((np_, bs), F32)

    sum_copy.wait()
    summed = (own_sum[...] + red_in[...]).astype(BF16)
    for b in range(ob):
        mine = summed[b * half : (b + 1) * half, :]
        far = tn(mine[:, :np_], bout_ref[b, 0:half, :]) + tn(mine[:, np_:], bout_ref[b, half:, :])
        out_ref[:, b * bs : (b + 1) * bs] = acc[h + b] + part[b] + far

    for copy in halo_out(side_fast, fast):
        copy.wait_send()
    for x in range(h):
        part_copy(side_fast, x, fast).wait_send()

    @pl.when(has_slow)
    def _():
        for copy in halo_out(side_slow, slow):
            copy.wait_send()
        for x in range(h):
            part_copy(side_slow, x, slow).wait_send()


def solution(mesh):
    n = mesh.shape["row"]

    def shards(coordinates, length_scale, probes, near_ids, near_count, basis_out, basis_in):
        ob, rank, bs = basis_out.shape
        np_ = probes.shape[0]
        own = ob * bs
        h = ob // 2
        slots = near_ids.shape[1]
        window = ob + 2 * h
        vmem = pl.BlockSpec(memory_space=pltpu.VMEM)
        dma = pltpu.SemaphoreType.DMA
        return pl.pallas_call(
            functools.partial(kernel, n, ob, bs),
            out_shape=jax.ShapeDtypeStruct((np_, own), F32),
            in_specs=[pl.BlockSpec(memory_space=pl.ANY)] * 6,
            out_specs=vmem,
            scratch_shapes=[
                pltpu.VMEM((3, own), F32),
                pltpu.VMEM((1, own), F32),
                pltpu.VMEM((ob, slots), jnp.int32),
                pltpu.VMEM((ob, rank, bs), BF16),
                pltpu.VMEM((ob, rank, bs), BF16),
                pltpu.VMEM((2, 3, h * bs), F32),
                pltpu.VMEM((2, 1, h * bs), F32),
                pltpu.VMEM((2, ob, slots), jnp.int32),
                pltpu.VMEM((np_, window * bs), BF16),
                pltpu.VMEM((ROWS, own), F32),
                pltpu.VMEM((window, ROWS, bs), F32),
                pltpu.VMEM((ob, ROWS, bs), F32),
                pltpu.VMEM((ob, bs, 8 * ROWS), BF16),
                pltpu.VMEM((window, 8 * ROWS, bs), BF16),
                pltpu.VMEM(((2 * HALO + 1) * window + 1, 1, bs), F32),
                pltpu.VMEM((window, np_, bs), F32),
                pltpu.VMEM((ob, np_, bs), F32),
                pltpu.VMEM((n // 2, ob * rank // 2, 2 * np_), BF16),
                pltpu.VMEM((n // 2, ob, 128), F32),
                pltpu.VMEM((ob, 128), F32),
                pltpu.VMEM((ob * rank // 2, 2 * np_), F32),
                pltpu.VMEM((ob * rank // 2, 2 * np_), F32),
                pltpu.VMEM((ob * rank // 2, 2 * np_), F32),
                pltpu.VMEM((2, bs, 2 * bs), F32),
                pltpu.VMEM((2, bs, bs), BF16),
                dma((6,)), dma((2, 4)), dma((2, 4)), dma((ob,)), dma((ob,)),
                dma((n // 4,)), dma((n // 4,)), dma((n // 4,)), dma((n // 4,)), dma((4,)), dma((4,)),
            ],
            compiler_params=pltpu.CompilerParams(collective_id=0, has_side_effects=True, vmem_limit_bytes=16 * 1024 * 1024),
        )(
            *[
                pltpu.with_memory_space_constraint(x, pltpu.HBM)
                for x in (coordinates, length_scale.reshape(1, own), probes, near_ids, basis_out, basis_in)
            ]
        )

    placed = (
        P(None, ("grp", "row")),
        P(("grp", "row")),
        P(None, ("grp", "row")),
        P(("grp", "row"), None),
        P(("grp", "row")),
        P(("grp", "row"), None, None),
        P(("grp", "row"), None, None),
    )
    return jax.shard_map(
        shards, mesh=mesh, in_specs=placed, out_specs=P(None, ("grp", "row")), check_vma=False
    )
```

```python
import functools
import math

import jax
import jax.numpy as jnp
from jax import lax
from jax.experimental import pallas as pl
from jax.experimental.pallas import tpu as pltpu
from jax.sharding import PartitionSpec as P

HALO = 8
ROWS = 8
OPEN_AT = 1
LEVEL_AT = 5
SUM_AT = 6
BEFORE = 3
STRIP = 16
LOG2E = 1.0 / math.log(2.0)
C_SCALE = math.log(2.0) ** (-2.0 / 3.0)
D_SCALE = 3.0 * LOG2E * LOG2E * C_SCALE
F32 = jnp.float32
BF16 = jnp.bfloat16


def split3(x):
    high = x.astype(BF16).astype(F32)
    rest = x - high
    mid = rest.astype(BF16).astype(F32)
    return high, mid, rest - mid


def left_stack(x):
    h, m, l = split3(x)
    return jnp.concatenate([h, h, m, h, l, m, m, l], axis=0)


def right_stack(x):
    h, m, l = split3(x)
    hm = jnp.concatenate([h, m], axis=0).astype(BF16)
    hl = jnp.concatenate([h, l], axis=0).astype(BF16)
    lm = jnp.concatenate([l, m], axis=0).astype(BF16)
    return jnp.concatenate([hm, hl, hm, lm], axis=0)


def matern(first, second):
    sq_dist = (first[0] - second[0]) * (first[0] - second[0])
    sq_dist = sq_dist + (first[1] - second[1]) * (first[1] - second[1])
    sq_dist = sq_dist + (first[2] - second[2]) * (first[2] - second[2])
    mean_sq = 0.5 * (first[3] * first[3] + second[3] * second[3])
    ratio = first[3] * second[3] / mean_sq
    prefac = ratio * jnp.sqrt(ratio)
    scaled = jnp.sqrt(3.0 * (sq_dist / mean_sq))
    return prefac * (1.0 + scaled) * jnp.exp(-scaled)


def nt(a, b):
    return lax.dot_general(a, b, (((1,), (1,)), ((), ())), preferred_element_type=F32)


def tn(a, b):
    return lax.dot_general(a, b, (((0,), (0,)), ((), ())), preferred_element_type=F32)


def nn(a, b):
    return lax.dot_general(a, b, (((1,), (0,)), ((), ())), preferred_element_type=F32)


def kernel(
    n, ob, bs,
    xyz_in, len_in, probes_in, ids_in, bout_in, bin_in, out_ref,
    xyz_ref, len_ref, ids_ref, bout_ref, bin_ref,
    xyz_h, len_h, ids_h, probes,
    rec_j, scale_j, cen_j, lhs, rhs_c, mask, acc, part,
    fold_all, cen_all, cen_y, own_sum, red_out, red_in,
    both, value_buf, kept, load_sem, halo_send, halo_recv, part_send, part_recv,
    gat_send, gat_recv, cen_send, cen_recv, low_send, low_recv,
):
    me = lax.axis_index("row")
    own = ob * bs
    h = ob // 2
    window = ob + 2 * h
    hb = h * bs
    quads = n // 4
    core = me % 2
    col_y = me // 2 % 2
    hi = me // 4
    fast = me + 1 - 2 * core
    slow = jnp.clip(me - 1 + 2 * core, 0, n - 1)
    has_left = me > 0
    has_right = me < n - 1
    has_slow = jnp.where(core == 0, has_left, has_right)
    across = me + 2 - 4 * col_y
    side_fast = 1 - core
    side_slow = core
    half = bin_ref.shape[1] // 2
    np_ = probes.shape[0]
    width = n // 2 * ob

    loads = [
        pltpu.make_async_copy(src, dst, load_sem.at[k])
        for k, (src, dst) in enumerate(
            (
                (xyz_in, xyz_ref), (len_in, len_ref), (ids_in, ids_ref),
                (probes_in, probes.at[:, hb : hb + own]), (bin_in, bin_ref), (bout_in, bout_ref),
            )
        )
    ]
    for load in loads:
        load.start()

    barrier = pltpu.get_barrier_semaphore()

    def greet(peer):
        pl.semaphore_signal(barrier, inc=1, device_id={"row": peer})

    greet(fast)
    pl.when(has_slow)(lambda: greet(slow))
    greet(across)

    def level(k):
        return lax.rem(hi + k, quads) * 4 + me % 4

    for k in range(1, quads):
        greet(level(k))

    def lanes(start, size):
        return pl.ds(start, size) if isinstance(start, int) else pl.ds(pl.multiple_of(start, size), size)

    def halo_out(side, peer):
        src = lanes(side * hb, hb)
        there = 1 - side
        pairs = (
            (xyz_in.at[:, src], xyz_h.at[there]),
            (len_in.at[:, src], len_h.at[there]),
            (ids_in, ids_h.at[there]),
            (probes_in.at[:, src], probes.at[:, lanes(there * (own + hb), hb)]),
        )
        return [
            pltpu.make_async_remote_copy(
                src_ref=a, dst_ref=b, send_sem=halo_send.at[side, k], recv_sem=halo_recv.at[there, k],
                device_id={"row": peer},
            )
            for k, (a, b) in enumerate(pairs)
        ]

    def halo_arrival(side, peer):
        pairs = (
            (xyz_in.at[:, 0:hb], xyz_h.at[side]),
            (len_in.at[:, 0:hb], len_h.at[side]),
            (ids_in, ids_h.at[side]),
            (probes_in.at[:, 0:hb], probes.at[:, lanes(side * (own + hb), hb)]),
        )
        return [
            pltpu.make_async_remote_copy(
                src_ref=a, dst_ref=b, send_sem=halo_send.at[side, k], recv_sem=halo_recv.at[side, k],
                device_id={"row": peer},
            )
            for k, (a, b) in enumerate(pairs)
        ]

    slot = core * quads + hi

    def level_copies(k, source):
        at = core * quads + source
        return [
            pltpu.make_async_remote_copy(
                src_ref=fold_all.at[at], dst_ref=fold_all.at[at],
                send_sem=gat_send.at[k], recv_sem=gat_recv.at[k], device_id={"row": level(k)},
            ),
            pltpu.make_async_remote_copy(
                src_ref=cen_all.at[at], dst_ref=cen_all.at[at],
                send_sem=cen_send.at[k], recv_sem=cen_recv.at[k], device_id={"row": level(k)},
            ),
        ]

    def core_copies(which):
        held = pl.ds(which * quads, quads)
        return [
            pltpu.make_async_remote_copy(
                src_ref=fold_all.at[held], dst_ref=fold_all.at[held],
                send_sem=low_send.at[0], recv_sem=low_recv.at[0], device_id={"row": fast},
            ),
            pltpu.make_async_remote_copy(
                src_ref=cen_all.at[held], dst_ref=cen_all.at[held],
                send_sem=low_send.at[1], recv_sem=low_recv.at[1], device_id={"row": fast},
            ),
        ]

    center_copy = pltpu.make_async_remote_copy(
        src_ref=cen_all.at[slot], dst_ref=cen_y,
        send_sem=low_send.at[2], recv_sem=low_recv.at[2], device_id={"row": across},
    )
    sum_copy = pltpu.make_async_remote_copy(
        src_ref=red_out, dst_ref=red_in,
        send_sem=low_send.at[3], recv_sem=low_recv.at[3], device_id={"row": across},
    )

    def part_copy(side, x, peer):
        return pltpu.make_async_remote_copy(
            src_ref=acc.at[(ob + h) * side + x], dst_ref=part.at[h * (1 - side) + x],
            send_sem=part_send.at[side * h + x], recv_sem=part_recv.at[h * (1 - side) + x],
            device_id={"row": peer},
        )

    def part_arrival(b, peer):
        return pltpu.make_async_remote_copy(
            src_ref=acc.at[b], dst_ref=part.at[b],
            send_sem=part_send.at[b], recv_sem=part_recv.at[b], device_id={"row": peer},
        )

    for load in loads[:5]:
        load.wait()
    row = lax.broadcasted_iota(jnp.int32, (ROWS, bs), 0)

    scale = jnp.where(row < 3, -2.0 * D_SCALE, jnp.where(row < 7, D_SCALE, 0.0))

    def fill_j(at, xyz, ln):
        rec_j[at, 0:3, :] = xyz
        rec_j[at, 3:6, :] = xyz
        rec_j[at, 6:7, :] = jnp.ones((1, bs), F32)
        rec_j[at, 7:8, :] = ln
        inv = 1.0 / ln
        scale_j[at] = scale * inv
        rhs_c[at] = right_stack((0.5 * C_SCALE) * jnp.where(row == 3, ln, jnp.where(row == 7, inv, 0.0)))

    ids = ids_ref[...]
    slots = ids.shape[1]
    lane = lax.broadcasted_iota(jnp.int32, (ROWS, 128), 1)
    own_centers = jnp.zeros((ROWS, 128), F32)
    for b in range(ob):
        ln = len_ref[:, b * bs : (b + 1) * bs]
        fill_j(h + b, xyz_ref[:, b * bs : (b + 1) * bs], ln)
        blk = rec_j[h + b]
        mean = jnp.sum(blk, axis=1, keepdims=True) * (1.0 / bs)
        own_centers = jnp.where(lane == b, mean, own_centers)
        cen = jnp.where(row < 6, jnp.broadcast_to(mean, (ROWS, bs)), 0.0)
        cen_j[b] = cen
        v = blk - cen
        norm = jnp.sum(jnp.where(row < 3, v * v, 0.0), axis=0, keepdims=True)
        feat = jnp.where(row < 3, v, jnp.where(row < 6, 1.0, norm)) * (1.0 / ln)
        lhs[b] = left_stack(jnp.where(row == 7, blk, feat)).T.astype(BF16)
        pb = probes[:, hb + b * bs : hb + (b + 1) * bs]
        fold = jnp.concatenate([nt(bin_ref[b, 0:half, :], pb), nt(bin_ref[b, half:, :], pb)], axis=1)
        fold_all[slot, b * half : (b + 1) * half, :] = fold.astype(BF16)
    square = jnp.concatenate([own_centers, jnp.zeros((128 - ROWS, 128), F32)], axis=0).T
    id_rows = jnp.concatenate(
        [jnp.zeros((ob, ROWS), F32), ids.astype(F32), jnp.zeros((ob, 128 - ROWS - slots), F32)], axis=1
    )
    own_cols = square[0:ob, :] + id_rows
    cen_all[slot] = own_cols

    acc[...] = jnp.zeros_like(acc)

    def member(ids, target):
        return jnp.max(jnp.where(ids == target, 1.0, 0.0), axis=1, keepdims=True)

    gid = lax.broadcasted_iota(jnp.int32, ids.shape, 0) + me * ob

    def mask_at(offset, q):
        return (offset + HALO) * window + q

    for offset in range(-HALO, HALO + 1):
        wide = jnp.broadcast_to(member(ids, gid + offset), (ob, bs))
        for b in range(ob):
            mask[mask_at(offset, h + b)] = wide[b : b + 1, :]
    blank = (2 * HALO + 1) * window
    mask[blank] = jnp.zeros((1, bs), F32)

    def right_side(o, q):
        v = rec_j[q] - cen_j[o]
        feat = jnp.where((row >= 3) & (row < 6), v * v, v) * scale_j[q]
        return jnp.concatenate([right_stack(feat), rhs_c[q]], axis=1)

    def entries(o, q, turn):
        both[turn] = nn(lhs[o], right_side(o, q))

    def values(turn, buf, s_at):
        for r in range(0, bs, STRIP):
            e = jnp.maximum(both[turn, r : r + STRIP, :bs], 1e-30)
            q = both[turn, r : r + STRIP, bs:]
            s = e * lax.rsqrt(e * q)
            buf[s_at, r : r + STRIP, :] = ((LOG2E + s) * jnp.exp2(-1.5 * lax.log2(q) - s)).astype(BF16)

    def forward(o, q, buf, s):
        p_q = probes[:, lanes(q * bs, bs)]
        acc[h + o] += mask[mask_at(q - h - o, h + o)] * nt(p_q, buf[s])

    def backward(o, q, buf, s):
        offset = q - h - o
        p_o = probes[:, lanes((h + o) * bs, bs)]
        acc[q] += mask[jnp.where(offset == 0, blank, mask_at(-offset, q))] * nn(p_o, buf[s])

    def finish(pairs, t, keep):
        if keep is None:
            forward(*pairs[t], value_buf, t % 2)
            backward(*pairs[t], value_buf, t % 2)
        else:
            backward(*pairs[t], kept, keep + t)

    def sweep(pairs, keep=None, old=None):
        entries(*pairs[0], 0)
        for t, pair in enumerate(pairs):
            if old:
                forward(*old[0][t], kept, old[1] + t)
            if t + 1 < len(pairs):
                entries(*pairs[t + 1], (t + 1) % 2)
            if keep is None:
                values(t % 2, value_buf, t % 2)
            else:
                values(t % 2, kept, keep + t)
            if t:
                finish(pairs, t - 1, keep)
        finish(pairs, len(pairs) - 1, keep)

    table = []
    for g in range(h):
        c = [(s + g) // ob for s in range(ob + 1)]
        first = [g + k * (ob - 1 - 2 * g) for k in c]
        table.append([(f, h + f + s - k * (ob - g)) for s, (k, f) in enumerate(zip(c, first))])
    for g in range(h // 2):
        cols = [(g, ob), (h - 1 - g, h)]
        table.append([(i, h + ob + c) for c, stop in cols for i in range(c, stop)])
    for g in range(h // 2):
        table.append([(c, i - h) for i in (h + g, ob - 1 - g) for c in range(h // 2, i + 1)])

    def open_links():
        pl.semaphore_wait(barrier, quads + 1 + jnp.where(has_slow, 1, 0))

        @pl.when(has_slow)
        def _():
            for copy in halo_out(side_slow, slow)[:3]:
                copy.start()

        for k in range(1, quads):
            for copy in level_copies(k, hi):
                copy.start()

        @pl.when(has_slow)
        def _():
            halo_out(side_slow, slow)[3].start()

        for copy in halo_out(side_fast, fast):
            copy.start()
        center_copy.start()

    def take_halo(side):
        first = side * (ob + h)
        for b in range(h):
            fill_j(first + b, xyz_h[side, :, b * bs : (b + 1) * bs], len_h[side, :, b * bs : (b + 1) * bs])
        there = ids_h[side]
        sign = 1 - 2 * side
        base = gid + (2 * side - 1) * ob
        for dj in range(1, HALO + 1):
            wide = jnp.broadcast_to(member(there, base + sign * dj), (ob, bs))
            for b in range(h):
                mask[mask_at(sign * dj, first + b)] = wide[(1 - side) * h + b : (1 - side) * h + b + 1, :]

    def take_fast(side):
        for copy in halo_arrival(side, fast):
            copy.wait_recv()
        take_halo(side)

    def take_slow(side):
        @pl.when(has_slow)
        def _():
            for copy in halo_arrival(side, slow)[:3]:
                copy.wait_recv()

        @pl.when(jnp.logical_not(has_slow))
        def _():
            xyz_h[side] = xyz_ref[:, 0:hb]
            len_h[side] = len_ref[:, 0:hb]
            ids_h[side] = ids_ref[...]
            probes[:, lanes(side * (own + hb), hb)] = probes[:, hb : 2 * hb]

        take_halo(side)

    def take_slow_probes(side):
        @pl.when(has_slow)
        def _():
            halo_arrival(side, slow)[3].wait_recv()

    def level_done():
        for k in range(1, quads):
            for copy in level_copies(k, hi):
                copy.wait()
        for copy in core_copies(core):
            copy.start()

    step_w = min(128, width)

    def partial_sums():
        for copy in core_copies(core):
            copy.wait()
        center_copy.wait()
        centers = cen_all[...].reshape(width, 128).T
        mine = cen_all[slot]
        column = lax.broadcasted_iota(jnp.int32, (ob, width), 1)
        holder = column // ob
        device = holder % quads * 4 + col_y * 2 + holder // quads
        global_ids = (device * ob + column % ob).astype(F32)
        picks = (0, 1, 2, 7)
        pick_r = lax.broadcasted_iota(jnp.int32, (step_w, step_w * half), 0)
        pick_c = lax.broadcasted_iota(jnp.int32, (step_w, step_w * half), 1)
        spread = jnp.where(pick_c // half == pick_r, 1.0, 0.0).astype(BF16)
        eye_r = lax.broadcasted_iota(jnp.int32, (ob * half, step_w * half), 0)
        eye_c = lax.broadcasted_iota(jnp.int32, (ob * half, step_w * half), 1)
        same = lax.rem(eye_r, half) == lax.rem(eye_c, half)
        per = step_w // ob
        totals = []
        for rows in (mine, cen_y[...]):
            coupling = matern([rows[:, c : c + 1] for c in picks], [centers[c : c + 1, :] for c in picks])
            near = jnp.zeros((ob, width), F32)
            for t in range(slots):
                near = jnp.where(rows[:, ROWS + t : ROWS + t + 1] == global_ids, 1.0, near)
            coupling = jnp.where(near > 0.0, 0.0, coupling).astype(BF16)
            total = jnp.zeros((ob * half, 2 * np_), F32)
            for q in range(width // step_w):
                wide = nn(coupling[:, q * step_w : (q + 1) * step_w], spread)
                wide = jnp.concatenate(
                    [jnp.broadcast_to(wide[i : i + 1, :], (half, step_w * half)) for i in range(ob)], axis=0
                )
                kron = jnp.where(same, wide, 0.0).astype(BF16)
                folded = fold_all[q * per : (q + 1) * per].reshape(step_w * half, 2 * np_)
                total = total + nn(kron, folded)
            totals.append(total)
        red_out[...] = totals[1]
        own_sum[...] = totals[0]
        sum_copy.start()

    before = min(BEFORE, h)
    there = before + h // 2
    common = {OPEN_AT: [open_links]}
    common.setdefault(LEVEL_AT, []).append(level_done)
    common.setdefault(SUM_AT, []).append(partial_sums)

    def rest(mine):
        at_slow = mine
        at_fast = 1 - mine

        def cross_tiles(side, k):
            return table[h + k] if side else table[h + h // 2 + k]

        for t in range(before, ob + 1):
            for hook in common.get(t, []):
                hook()
            if t == ob:
                break
            k = t - before if t < there else t - there
            if t == before:
                take_slow(at_slow)
            if t == there:
                take_slow_probes(at_slow)
                take_fast(at_fast)
            if t < there:
                sweep(cross_tiles(at_slow, k), keep=k * (ob + 1))
            elif t < before + h:
                sweep(cross_tiles(at_fast, k), old=(cross_tiles(at_slow, k), k * (ob + 1)))
            else:
                sweep(table[t - h])
            if t < before + h:
                side = at_slow if t < there else at_fast
                peer = slow if t < there else fast

                def send(side=side, peer=peer, k=k):
                    part_copy(side, k, peer).start()
                    part_copy(side, h - 1 - k, peer).start()

                if t < there:
                    pl.when(has_slow)(send)
                else:
                    send()

    for t in range(before):
        for hook in common.get(t, []):
            hook()
        sweep(table[t])
    for c in range(2):
        pl.when(core == c)(functools.partial(rest, c))

    loads[5].wait()

    for x in range(h):
        part_arrival(side_fast * h + x, fast).wait_recv()

    @pl.when(has_slow)
    def _():
        for x in range(h):
            part_arrival(side_slow * h + x, slow).wait_recv()

    @pl.when(jnp.logical_not(has_slow))
    def _():
        for x in range(h):
            part[side_slow * h + x] = jnp.zeros((np_, bs), F32)

    sum_copy.wait()
    summed = (own_sum[...] + red_in[...]).astype(BF16)
    for b in range(ob):
        mine = summed[b * half : (b + 1) * half, :]
        far = tn(mine[:, :np_], bout_ref[b, 0:half, :]) + tn(mine[:, np_:], bout_ref[b, half:, :])
        out_ref[:, b * bs : (b + 1) * bs] = acc[h + b] + part[b] + far

    for copy in halo_out(side_fast, fast):
        copy.wait_send()
    for x in range(h):
        part_copy(side_fast, x, fast).wait_send()

    @pl.when(has_slow)
    def _():
        for copy in halo_out(side_slow, slow):
            copy.wait_send()
        for x in range(h):
            part_copy(side_slow, x, slow).wait_send()


def solution(mesh):
    n = mesh.shape["row"]

    def shards(coordinates, length_scale, probes, near_ids, near_count, basis_out, basis_in):
        ob, rank, bs = basis_out.shape
        np_ = probes.shape[0]
        own = ob * bs
        h = ob // 2
        slots = near_ids.shape[1]
        window = ob + 2 * h
        vmem = pl.BlockSpec(memory_space=pltpu.VMEM)
        dma = pltpu.SemaphoreType.DMA
        return pl.pallas_call(
            functools.partial(kernel, n, ob, bs),
            out_shape=jax.ShapeDtypeStruct((np_, own), F32),
            in_specs=[pl.BlockSpec(memory_space=pl.ANY)] * 6,
            out_specs=vmem,
            scratch_shapes=[
                pltpu.VMEM((3, own), F32),
                pltpu.VMEM((1, own), F32),
                pltpu.VMEM((ob, slots), jnp.int32),
                pltpu.VMEM((ob, rank, bs), BF16),
                pltpu.VMEM((ob, rank, bs), BF16),
                pltpu.VMEM((2, 3, h * bs), F32),
                pltpu.VMEM((2, 1, h * bs), F32),
                pltpu.VMEM((2, ob, slots), jnp.int32),
                pltpu.VMEM((np_, window * bs), BF16),
                pltpu.VMEM((window, ROWS, bs), F32),
                pltpu.VMEM((window, ROWS, bs), F32),
                pltpu.VMEM((ob, ROWS, bs), F32),
                pltpu.VMEM((ob, bs, 8 * ROWS), BF16),
                pltpu.VMEM((window, 8 * ROWS, bs), BF16),
                pltpu.VMEM(((2 * HALO + 1) * window + 1, 1, bs), F32),
                pltpu.VMEM((window, np_, bs), F32),
                pltpu.VMEM((ob, np_, bs), F32),
                pltpu.VMEM((n // 2, ob * rank // 2, 2 * np_), BF16),
                pltpu.VMEM((n // 2, ob, 128), F32),
                pltpu.VMEM((ob, 128), F32),
                pltpu.VMEM((ob * rank // 2, 2 * np_), F32),
                pltpu.VMEM((ob * rank // 2, 2 * np_), F32),
                pltpu.VMEM((ob * rank // 2, 2 * np_), F32),
                pltpu.VMEM((2, bs, 2 * bs), F32),
                pltpu.VMEM((2, bs, bs), BF16),
                pltpu.VMEM((h // 2 * (ob + 1), bs, bs), BF16),
                dma((6,)), dma((2, 4)), dma((2, 4)), dma((ob,)), dma((ob,)),
                dma((n // 4,)), dma((n // 4,)), dma((n // 4,)), dma((n // 4,)), dma((4,)), dma((4,)),
            ],
            compiler_params=pltpu.CompilerParams(collective_id=0, has_side_effects=True, vmem_limit_bytes=16 * 1024 * 1024),
        )(
            *[
                pltpu.with_memory_space_constraint(x, pltpu.HBM)
                for x in (coordinates, length_scale.reshape(1, own), probes, near_ids, basis_out, basis_in)
            ]
        )

    placed = (
        P(None, ("grp", "row")),
        P(("grp", "row")),
        P(None, ("grp", "row")),
        P(("grp", "row"), None),
        P(("grp", "row")),
        P(("grp", "row"), None, None),
        P(("grp", "row"), None, None),
    )
    return jax.shard_map(
        shards, mesh=mesh, in_specs=placed, out_specs=P(None, ("grp", "row")), check_vma=False
    )
```

```python
import functools
import math

import jax
import jax.numpy as jnp
from jax import lax
from jax.experimental import pallas as pl
from jax.experimental.pallas import tpu as pltpu
from jax.sharding import PartitionSpec as P

HALO = 8
ROWS = 8
OPEN_TILE = 11
LEVEL_TILE = 14
SUM_TILE = 4
BEFORE = 3
STRIP = 16
LOG2E = 1.0 / math.log(2.0)
C_SCALE = math.log(2.0) ** (-2.0 / 3.0)
D_SCALE = 3.0 * LOG2E * LOG2E * C_SCALE
F32 = jnp.float32
BF16 = jnp.bfloat16


def split3(x):
    high = x.astype(BF16).astype(F32)
    rest = x - high
    mid = rest.astype(BF16).astype(F32)
    return high, mid, rest - mid


def left_stack(x):
    h, m, l = split3(x)
    return jnp.concatenate([h, h, m, h, l, m, m, l], axis=0)


def right_stack(x):
    h, m, l = split3(x)
    hm = jnp.concatenate([h, m], axis=0).astype(BF16)
    hl = jnp.concatenate([h, l], axis=0).astype(BF16)
    lm = jnp.concatenate([l, m], axis=0).astype(BF16)
    return jnp.concatenate([hm, hl, hm, lm], axis=0)


def matern(first, second):
    sq_dist = (first[0] - second[0]) * (first[0] - second[0])
    sq_dist = sq_dist + (first[1] - second[1]) * (first[1] - second[1])
    sq_dist = sq_dist + (first[2] - second[2]) * (first[2] - second[2])
    mean_sq = 0.5 * (first[3] * first[3] + second[3] * second[3])
    ratio = first[3] * second[3] / mean_sq
    prefac = ratio * jnp.sqrt(ratio)
    scaled = jnp.sqrt(3.0 * (sq_dist / mean_sq))
    return prefac * (1.0 + scaled) * jnp.exp(-scaled)


def nt(a, b):
    return lax.dot_general(a, b, (((1,), (1,)), ((), ())), preferred_element_type=F32)


def tn(a, b):
    return lax.dot_general(a, b, (((0,), (0,)), ((), ())), preferred_element_type=F32)


def nn(a, b):
    return lax.dot_general(a, b, (((1,), (0,)), ((), ())), preferred_element_type=F32)


def kernel(
    n, ob, bs,
    xyz_in, len_in, probes_in, ids_in, bout_in, bin_in, out_ref,
    xyz_ref, len_ref, ids_ref, bout_ref, bin_ref,
    xyz_h, len_h, ids_h, probes,
    rec_j, scale_j, cen_j, lhs, rhs_c, mask, acc, part,
    fold_all, cen_all, cen_y, own_sum, red_out, red_in,
    both, value_buf, kept, load_sem, halo_send, halo_recv, part_send, part_recv,
    gat_send, gat_recv, cen_send, cen_recv, low_send, low_recv,
):
    me = lax.axis_index("row")
    own = ob * bs
    h = ob // 2
    window = ob + 2 * h
    hb = h * bs
    quads = n // 4
    core = me % 2
    col_y = me // 2 % 2
    hi = me // 4
    fast = me + 1 - 2 * core
    slow = jnp.clip(me - 1 + 2 * core, 0, n - 1)
    has_left = me > 0
    has_right = me < n - 1
    has_slow = jnp.where(core == 0, has_left, has_right)
    across = me + 2 - 4 * col_y
    side_fast = 1 - core
    side_slow = core
    half = bin_ref.shape[1] // 2
    np_ = probes.shape[0]
    width = n // 2 * ob

    loads = [
        pltpu.make_async_copy(src, dst, load_sem.at[k])
        for k, (src, dst) in enumerate(
            (
                (xyz_in, xyz_ref), (len_in, len_ref), (ids_in, ids_ref),
                (probes_in, probes.at[:, hb : hb + own]), (bin_in, bin_ref), (bout_in, bout_ref),
            )
        )
    ]
    for load in loads:
        load.start()

    barrier = pltpu.get_barrier_semaphore()

    def greet(peer):
        pl.semaphore_signal(barrier, inc=1, device_id={"row": peer})

    greet(fast)
    pl.when(has_slow)(lambda: greet(slow))
    greet(across)

    def level(k):
        return lax.rem(hi + k, quads) * 4 + me % 4

    for k in range(1, quads):
        greet(level(k))

    def lanes(start, size):
        return pl.ds(start, size) if isinstance(start, int) else pl.ds(pl.multiple_of(start, size), size)

    def halo_out(side, peer):
        src = lanes(side * hb, hb)
        there = 1 - side
        pairs = (
            (xyz_in.at[:, src], xyz_h.at[there]),
            (len_in.at[:, src], len_h.at[there]),
            (ids_in, ids_h.at[there]),
            (probes_in.at[:, src], probes.at[:, lanes(there * (own + hb), hb)]),
        )
        return [
            pltpu.make_async_remote_copy(
                src_ref=a, dst_ref=b, send_sem=halo_send.at[side, k], recv_sem=halo_recv.at[there, k],
                device_id={"row": peer},
            )
            for k, (a, b) in enumerate(pairs)
        ]

    def halo_arrival(side, peer):
        pairs = (
            (xyz_in.at[:, 0:hb], xyz_h.at[side]),
            (len_in.at[:, 0:hb], len_h.at[side]),
            (ids_in, ids_h.at[side]),
            (probes_in.at[:, 0:hb], probes.at[:, lanes(side * (own + hb), hb)]),
        )
        return [
            pltpu.make_async_remote_copy(
                src_ref=a, dst_ref=b, send_sem=halo_send.at[side, k], recv_sem=halo_recv.at[side, k],
                device_id={"row": peer},
            )
            for k, (a, b) in enumerate(pairs)
        ]

    slot = core * quads + hi

    def level_copies(k, source):
        at = core * quads + source
        return [
            pltpu.make_async_remote_copy(
                src_ref=fold_all.at[at], dst_ref=fold_all.at[at],
                send_sem=gat_send.at[k], recv_sem=gat_recv.at[k], device_id={"row": level(k)},
            ),
            pltpu.make_async_remote_copy(
                src_ref=cen_all.at[at], dst_ref=cen_all.at[at],
                send_sem=cen_send.at[k], recv_sem=cen_recv.at[k], device_id={"row": level(k)},
            ),
        ]

    def core_copies(which):
        held = pl.ds(which * quads, quads)
        return [
            pltpu.make_async_remote_copy(
                src_ref=fold_all.at[held], dst_ref=fold_all.at[held],
                send_sem=low_send.at[0], recv_sem=low_recv.at[0], device_id={"row": fast},
            ),
            pltpu.make_async_remote_copy(
                src_ref=cen_all.at[held], dst_ref=cen_all.at[held],
                send_sem=low_send.at[1], recv_sem=low_recv.at[1], device_id={"row": fast},
            ),
        ]

    center_copy = pltpu.make_async_remote_copy(
        src_ref=cen_all.at[slot], dst_ref=cen_y,
        send_sem=low_send.at[2], recv_sem=low_recv.at[2], device_id={"row": across},
    )
    sum_copy = pltpu.make_async_remote_copy(
        src_ref=red_out, dst_ref=red_in,
        send_sem=low_send.at[3], recv_sem=low_recv.at[3], device_id={"row": across},
    )

    def part_copy(side, x, peer, there=None):
        there = h * (1 - side) + x if there is None else there
        return pltpu.make_async_remote_copy(
            src_ref=acc.at[(ob + h) * side + x], dst_ref=part.at[there],
            send_sem=part_send.at[side * h + x], recv_sem=part_recv.at[there],
            device_id={"row": peer},
        )

    def slow_part(side, x):
        return part_copy(
            side, x, jnp.where(has_slow, slow, fast), jnp.where(has_slow, h * (1 - side) + x, ob + x)
        )

    def part_arrival(b, peer):
        return pltpu.make_async_remote_copy(
            src_ref=acc.at[b], dst_ref=part.at[b],
            send_sem=part_send.at[b], recv_sem=part_recv.at[b], device_id={"row": peer},
        )

    for load in loads[:2]:
        load.wait()
    row = lax.broadcasted_iota(jnp.int32, (ROWS, bs), 0)

    scale = jnp.where(row < 3, -2.0 * D_SCALE, jnp.where(row < 7, D_SCALE, 0.0))

    def fill_j(at, xyz, ln):
        rec_j[at, 0:3, :] = xyz
        rec_j[at, 3:6, :] = xyz
        rec_j[at, 6:7, :] = jnp.ones((1, bs), F32)
        rec_j[at, 7:8, :] = ln
        inv = 1.0 / ln
        scale_j[at] = scale * inv
        rhs_c[at] = right_stack((0.5 * C_SCALE) * jnp.where(row == 3, ln, jnp.where(row == 7, inv, 0.0)))

    lane = lax.broadcasted_iota(jnp.int32, (ROWS, 128), 1)
    own_centers = jnp.zeros((ROWS, 128), F32)
    for b in range(ob):
        ln = len_ref[:, b * bs : (b + 1) * bs]
        fill_j(h + b, xyz_ref[:, b * bs : (b + 1) * bs], ln)
        blk = rec_j[h + b]
        mean = jnp.sum(blk, axis=1, keepdims=True) * (1.0 / bs)
        own_centers = jnp.where(lane == b, mean, own_centers)
        cen = jnp.where(row < 6, jnp.broadcast_to(mean, (ROWS, bs)), 0.0)
        cen_j[b] = cen
        v = blk - cen
        norm = jnp.sum(jnp.where(row < 3, v * v, 0.0), axis=0, keepdims=True)
        feat = jnp.where(row < 3, v, jnp.where(row < 6, 1.0, norm)) * (1.0 / ln)
        lhs[b] = left_stack(jnp.where(row == 7, blk, feat)).T.astype(BF16)
    for load in loads[2:5]:
        load.wait()
    ids = ids_ref[...]
    slots = ids.shape[1]
    for b in range(ob):
        pb = probes[:, hb + b * bs : hb + (b + 1) * bs]
        fold = jnp.concatenate([nt(bin_ref[b, 0:half, :], pb), nt(bin_ref[b, half:, :], pb)], axis=1)
        fold_all[slot, b * half : (b + 1) * half, :] = fold.astype(BF16)
    square = jnp.concatenate([own_centers, jnp.zeros((128 - ROWS, 128), F32)], axis=0).T
    id_rows = jnp.concatenate(
        [jnp.zeros((ob, ROWS), F32), ids.astype(F32), jnp.zeros((ob, 128 - ROWS - slots), F32)], axis=1
    )
    own_cols = square[0:ob, :] + id_rows
    cen_all[slot] = own_cols

    def member(ids, target):
        return jnp.max(jnp.where(ids == target, 1.0, 0.0), axis=1, keepdims=True)

    gid = lax.broadcasted_iota(jnp.int32, ids.shape, 0) + me * ob

    def mask_at(offset, q):
        return (offset + HALO) * window + q

    for offset in range(-HALO, HALO + 1):
        wide = jnp.broadcast_to(member(ids, gid + offset), (ob, bs))
        for b in range(ob):
            mask[mask_at(offset, h + b)] = wide[b : b + 1, :]

    def right_side(o, q):
        v = rec_j[q] - cen_j[o]
        feat = jnp.where((row >= 3) & (row < 6), v * v, v) * scale_j[q]
        return jnp.concatenate([right_stack(feat), rhs_c[q]], axis=1)

    def entries(o, q, turn):
        both[turn] = nn(lhs[o], right_side(o, q))

    def values(turn, buf, s_at):
        for r in range(0, bs, STRIP):
            e = jnp.maximum(both[turn, r : r + STRIP, :bs], 1e-30)
            q = both[turn, r : r + STRIP, bs:]
            s = e * lax.rsqrt(e * q)
            buf[s_at, r : r + STRIP, :] = ((LOG2E + s) * jnp.exp2(-1.5 * lax.log2(q) - s)).astype(BF16)

    def add(at, value, seen):
        if at in seen:
            acc[at] += value
        else:
            acc[at] = value
            seen.add(at)

    def forward(o, q, buf, s, seen):
        p_q = probes[:, lanes(q * bs, bs)]
        add(h + o, mask[mask_at(q - h - o, h + o)] * nt(p_q, buf[s]), seen)

    def backward(o, q, buf, s, seen):
        if q != h + o:
            p_o = probes[:, lanes((h + o) * bs, bs)]
            add(q, mask[mask_at(h + o - q, q)] * nn(p_o, buf[s]), seen)

    def finish(pairs, t, keep, seen):
        if keep is None:
            forward(*pairs[t], value_buf, t % 2, seen)
            backward(*pairs[t], value_buf, t % 2, seen)
        else:
            backward(*pairs[t], kept, keep + t, seen)

    def sweep(pairs, seen, keep=None, old=None, after={}):
        entries(*pairs[0], 0)
        for t, pair in enumerate(pairs):
            if old:
                forward(*old[0][t], kept, old[1] + t, seen)
            if t + 1 < len(pairs):
                entries(*pairs[t + 1], (t + 1) % 2)
            if keep is None:
                values(t % 2, value_buf, t % 2)
            else:
                values(t % 2, kept, keep + t)
            if t:
                finish(pairs, t - 1, keep, seen)
                for hook in after.get(t - 1, ()):
                    hook()
        finish(pairs, len(pairs) - 1, keep, seen)
        for hook in after.get(len(pairs) - 1, ()):
            hook()

    table = []
    for g in range(h):
        c = [(s + g) // ob for s in range(ob + 1)]
        first = [g + k * (ob - 1 - 2 * g) for k in c]
        table.append([(f, h + f + s - k * (ob - g)) for s, (k, f) in enumerate(zip(c, first))])
    for g in range(h // 2):
        cols = [(g, ob), (h - 1 - g, h)]
        table.append([(i, h + ob + c) for c, stop in cols for i in range(c, stop)])
    for g in range(h // 2):
        table.append([(c, i - h) for i in (h + g, ob - 1 - g) for c in range(h // 2, i + 1)])

    left_groups = [(i, [(c, i) for c in range(h // 2, h + i + 1)]) for i in range(h)]
    right_groups = [(c, [(i, h + ob + c) for i in range(c, ob if c < h // 2 else h)]) for c in reversed(range(h))]
    right_groups.sort(key=lambda group: len(group[1]))
    slow_groups = (left_groups, right_groups)

    def open_links():
        pl.semaphore_wait(barrier, quads + 1 + jnp.where(has_slow, 1, 0))

        @pl.when(has_slow)
        def _():
            for copy in halo_out(side_slow, slow)[:3]:
                copy.start()

        for k in range(1, quads):
            for copy in level_copies(k, hi):
                copy.start()

        @pl.when(has_slow)
        def _():
            halo_out(side_slow, slow)[3].start()

        for copy in halo_out(side_fast, fast):
            copy.start()
        center_copy.start()

    def take_halo(side):
        first = side * (ob + h)
        for b in range(h):
            fill_j(first + b, xyz_h[side, :, b * bs : (b + 1) * bs], len_h[side, :, b * bs : (b + 1) * bs])
        there = ids_h[side]
        sign = 1 - 2 * side
        base = gid + (2 * side - 1) * ob
        for dj in range(1, HALO + 1):
            wide = jnp.broadcast_to(member(there, base + sign * dj), (ob, bs))
            for b in range(h):
                mask[mask_at(sign * dj, first + b)] = wide[(1 - side) * h + b : (1 - side) * h + b + 1, :]

    def take_fast(side):
        for copy in halo_arrival(side, fast):
            copy.wait_recv()
        take_halo(side)

    def take_slow(side):
        @pl.when(has_slow)
        def _():
            for copy in halo_arrival(side, slow)[:3]:
                copy.wait_recv()

        @pl.when(jnp.logical_not(has_slow))
        def _():
            xyz_h[side] = xyz_ref[:, 0:hb]
            len_h[side] = len_ref[:, 0:hb]
            ids_h[side] = ids_ref[...]
            probes[:, lanes(side * (own + hb), hb)] = probes[:, hb : 2 * hb]

        take_halo(side)

    def take_slow_probes(side):
        @pl.when(has_slow)
        def _():
            halo_arrival(side, slow)[3].wait_recv()

    def level_done():
        for k in range(1, quads):
            for copy in level_copies(k, hi):
                copy.wait()
        for copy in core_copies(core):
            copy.start()

    step_w = min(128, width)

    def partial_sums():
        for copy in core_copies(core):
            copy.wait()
        center_copy.wait()
        centers = cen_all[...].reshape(width, 128).T
        mine = cen_all[slot]
        column = lax.broadcasted_iota(jnp.int32, (ob, width), 1)
        holder = column // ob
        device = holder % quads * 4 + col_y * 2 + holder // quads
        global_ids = (device * ob + column % ob).astype(F32)
        picks = (0, 1, 2, 7)
        pick_r = lax.broadcasted_iota(jnp.int32, (step_w, step_w * half), 0)
        pick_c = lax.broadcasted_iota(jnp.int32, (step_w, step_w * half), 1)
        spread = jnp.where(pick_c // half == pick_r, 1.0, 0.0).astype(BF16)
        eye_r = lax.broadcasted_iota(jnp.int32, (ob * half, step_w * half), 0)
        eye_c = lax.broadcasted_iota(jnp.int32, (ob * half, step_w * half), 1)
        same = lax.rem(eye_r, half) == lax.rem(eye_c, half)
        per = step_w // ob
        totals = []
        for rows in (mine, cen_y[...]):
            coupling = matern([rows[:, c : c + 1] for c in picks], [centers[c : c + 1, :] for c in picks])
            near = jnp.zeros((ob, width), F32)
            for t in range(slots):
                near = jnp.where(rows[:, ROWS + t : ROWS + t + 1] == global_ids, 1.0, near)
            coupling = jnp.where(near > 0.0, 0.0, coupling).astype(BF16)
            total = jnp.zeros((ob * half, 2 * np_), F32)
            for q in range(width // step_w):
                wide = nn(coupling[:, q * step_w : (q + 1) * step_w], spread)
                wide = jnp.concatenate(
                    [jnp.broadcast_to(wide[i : i + 1, :], (half, step_w * half)) for i in range(ob)], axis=0
                )
                kron = jnp.where(same, wide, 0.0).astype(BF16)
                folded = fold_all[q * per : (q + 1) * per].reshape(step_w * half, 2 * np_)
                total = total + nn(kron, folded)
            totals.append(total)
        red_out[...] = totals[1]
        own_sum[...] = totals[0]
        sum_copy.start()

    before = min(BEFORE, h)
    there = before + h // 2

    def rest(mine):
        at_slow = mine
        at_fast = 1 - mine
        seen = set(touched)

        slow_tiles = [tile for _, tiles in slow_groups[at_slow] for tile in tiles]

        def cross_tiles(side, k):
            return table[h + k] if side else table[h + h // 2 + k]

        for t in range(before, ob):
            if t == before:
                take_slow(at_slow)
                after, count = {}, 0
                for x, tiles in slow_groups[at_slow]:
                    count += len(tiles)
                    after[count - 1] = [lambda x=x: slow_part(at_slow, x).start()]
                after.setdefault(min(LEVEL_TILE, count - 1), []).append(level_done)
                sweep(slow_tiles, seen, keep=0, after=after)
            if t == there:
                take_slow_probes(at_slow)
                take_fast(at_fast)
            if t >= there:
                if t < before + h:
                    k = t - there
                    at = k * (ob + 1)
                    after = {min(SUM_TILE, ob): [partial_sums]} if k == 0 else {}
                    sweep(cross_tiles(at_fast, k), seen, old=(slow_tiles[at : at + ob + 1], at), after=after)
                    part_copy(at_fast, k, fast).start()
                    part_copy(at_fast, h - 1 - k, fast).start()
                else:
                    sweep(table[t - h], seen)

    early = [tile for tiles in table[:before] for tile in tiles]
    touched = set()
    sweep(early[:OPEN_TILE], touched)
    open_links()
    sweep(early[OPEN_TILE:], touched)
    for c in range(2):
        pl.when(core == c)(functools.partial(rest, c))

    loads[5].wait()

    for x in range(h):
        part_arrival(side_fast * h + x, fast).wait_recv()

    @pl.when(has_slow)
    def _():
        for x in range(h):
            part_arrival(side_slow * h + x, slow).wait_recv()

    @pl.when(jnp.logical_not(has_slow))
    def _():
        for x in range(h):
            part[side_slow * h + x] = jnp.zeros((np_, bs), F32)

    sum_copy.wait()
    summed = (own_sum[...] + red_in[...]).astype(BF16)
    for b in range(ob):
        mine = summed[b * half : (b + 1) * half, :]
        far = tn(mine[:, :np_], bout_ref[b, 0:half, :]) + tn(mine[:, np_:], bout_ref[b, half:, :])
        out_ref[:, b * bs : (b + 1) * bs] = acc[h + b] + part[b] + far

    for copy in halo_out(side_fast, fast):
        copy.wait_send()
    for x in range(h):
        part_copy(side_fast, x, fast).wait_send()

    @pl.when(has_slow)
    def _():
        for copy in halo_out(side_slow, slow):
            copy.wait_send()

    for x in range(h):
        slow_part(side_slow, x).wait_send()

    @pl.when(jnp.logical_or(me == 1, me == n - 2))
    def _():
        for x in range(h):
            part_arrival(ob + x, fast).wait_recv()


def solution(mesh):
    n = mesh.shape["row"]

    def shards(coordinates, length_scale, probes, near_ids, near_count, basis_out, basis_in):
        ob, rank, bs = basis_out.shape
        np_ = probes.shape[0]
        own = ob * bs
        h = ob // 2
        slots = near_ids.shape[1]
        window = ob + 2 * h
        vmem = pl.BlockSpec(memory_space=pltpu.VMEM)
        dma = pltpu.SemaphoreType.DMA
        return pl.pallas_call(
            functools.partial(kernel, n, ob, bs),
            out_shape=jax.ShapeDtypeStruct((np_, own), F32),
            in_specs=[pl.BlockSpec(memory_space=pl.ANY)] * 6,
            out_specs=vmem,
            scratch_shapes=[
                pltpu.VMEM((3, own), F32),
                pltpu.VMEM((1, own), F32),
                pltpu.VMEM((ob, slots), jnp.int32),
                pltpu.VMEM((ob, rank, bs), BF16),
                pltpu.VMEM((ob, rank, bs), BF16),
                pltpu.VMEM((2, 3, h * bs), F32),
                pltpu.VMEM((2, 1, h * bs), F32),
                pltpu.VMEM((2, ob, slots), jnp.int32),
                pltpu.VMEM((np_, window * bs), BF16),
                pltpu.VMEM((window, ROWS, bs), F32),
                pltpu.VMEM((window, ROWS, bs), F32),
                pltpu.VMEM((ob, ROWS, bs), F32),
                pltpu.VMEM((ob, bs, 8 * ROWS), BF16),
                pltpu.VMEM((window, 8 * ROWS, bs), BF16),
                pltpu.VMEM(((2 * HALO + 1) * window, 1, bs), F32),
                pltpu.VMEM((window, np_, bs), F32),
                pltpu.VMEM((ob + h, np_, bs), F32),
                pltpu.VMEM((n // 2, ob * rank // 2, 2 * np_), BF16),
                pltpu.VMEM((n // 2, ob, 128), F32),
                pltpu.VMEM((ob, 128), F32),
                pltpu.VMEM((ob * rank // 2, 2 * np_), F32),
                pltpu.VMEM((ob * rank // 2, 2 * np_), F32),
                pltpu.VMEM((ob * rank // 2, 2 * np_), F32),
                pltpu.VMEM((2, bs, 2 * bs), F32),
                pltpu.VMEM((2, bs, bs), BF16),
                pltpu.VMEM((h // 2 * (ob + 1), bs, bs), BF16),
                dma((6,)), dma((2, 4)), dma((2, 4)), dma((ob + h,)), dma((ob + h,)),
                dma((n // 4,)), dma((n // 4,)), dma((n // 4,)), dma((n // 4,)), dma((4,)), dma((4,)),
            ],
            compiler_params=pltpu.CompilerParams(collective_id=0, has_side_effects=True, vmem_limit_bytes=16 * 1024 * 1024),
        )(
            *[
                pltpu.with_memory_space_constraint(x, pltpu.HBM)
                for x in (coordinates, length_scale.reshape(1, own), probes, near_ids, basis_out, basis_in)
            ]
        )

    placed = (
        P(None, ("grp", "row")),
        P(("grp", "row")),
        P(None, ("grp", "row")),
        P(("grp", "row"), None),
        P(("grp", "row")),
        P(("grp", "row"), None, None),
        P(("grp", "row"), None, None),
    )
    return jax.shard_map(
        shards, mesh=mesh, in_specs=placed, out_specs=P(None, ("grp", "row")), check_vma=False
    )
```

```python
import functools
import math

import jax
import jax.numpy as jnp
from jax import lax
from jax.experimental import pallas as pl
from jax.experimental.pallas import tpu as pltpu
from jax.sharding import PartitionSpec as P

HALO = 8
ROWS = 8
OPEN_TILE = 12
LEVEL_TILE = 14
SUM_TILE = 3
BEFORE = 3
STRIP = 16
LOG2E = 1.0 / math.log(2.0)
C_SCALE = math.log(2.0) ** (-2.0 / 3.0)
D_SCALE = 3.0 * LOG2E * LOG2E * C_SCALE
F32 = jnp.float32
BF16 = jnp.bfloat16


def split3(x):
    high = x.astype(BF16).astype(F32)
    rest = x - high
    mid = rest.astype(BF16).astype(F32)
    return high, mid, rest - mid


def left_stack(x):
    h, m, l = split3(x)
    return jnp.concatenate([h, h, m, h, l, m, m, l], axis=0)


def right_stack(x):
    h, m, l = split3(x)
    hm = jnp.concatenate([h, m], axis=0).astype(BF16)
    hl = jnp.concatenate([h, l], axis=0).astype(BF16)
    lm = jnp.concatenate([l, m], axis=0).astype(BF16)
    return jnp.concatenate([hm, hl, hm, lm], axis=0)


def matern(first, second):
    sq_dist = (first[0] - second[0]) * (first[0] - second[0])
    sq_dist = sq_dist + (first[1] - second[1]) * (first[1] - second[1])
    sq_dist = sq_dist + (first[2] - second[2]) * (first[2] - second[2])
    mean_sq = 0.5 * (first[3] * first[3] + second[3] * second[3])
    ratio = first[3] * second[3] / mean_sq
    prefac = ratio * jnp.sqrt(ratio)
    scaled = jnp.sqrt(3.0 * (sq_dist / mean_sq))
    return prefac * (1.0 + scaled) * jnp.exp(-scaled)


def nt(a, b):
    return lax.dot_general(a, b, (((1,), (1,)), ((), ())), preferred_element_type=F32)


def tn(a, b):
    return lax.dot_general(a, b, (((0,), (0,)), ((), ())), preferred_element_type=F32)


def nn(a, b):
    return lax.dot_general(a, b, (((1,), (0,)), ((), ())), preferred_element_type=F32)


def kernel(
    n, ob, bs,
    xyz_in, len_in, probes_in, ids_in, bout_in, bin_in, out_ref,
    xyz_ref, len_ref, ids_ref, bout_ref, bin_ref,
    xyz_h, len_h, ids_h, probes,
    rec_j, scale_j, cen_j, lhs, rhs_c, mask, acc, part,
    fold_all, cen_all, cen_y, own_sum, red_out, red_in,
    both, value_buf, kept, load_sem, halo_send, halo_recv, part_send, part_recv,
    gat_send, gat_recv, cen_send, cen_recv, low_send, low_recv,
):
    me = lax.axis_index("row")
    own = ob * bs
    h = ob // 2
    window = ob + 2 * h
    hb = h * bs
    quads = n // 4
    core = me % 2
    col_y = me // 2 % 2
    hi = me // 4
    fast = me + 1 - 2 * core
    slow = jnp.clip(me - 1 + 2 * core, 0, n - 1)
    has_left = me > 0
    has_right = me < n - 1
    has_slow = jnp.where(core == 0, has_left, has_right)
    across = me + 2 - 4 * col_y
    side_fast = 1 - core
    side_slow = core
    half = bin_ref.shape[1] // 2
    np_ = probes.shape[0]
    width = n // 2 * ob

    loads = [
        pltpu.make_async_copy(src, dst, load_sem.at[k])
        for k, (src, dst) in enumerate(
            (
                (xyz_in, xyz_ref), (len_in, len_ref), (ids_in, ids_ref),
                (probes_in, probes.at[:, hb : hb + own]), (bin_in, bin_ref), (bout_in, bout_ref),
            )
        )
    ]
    for load in loads:
        load.start()

    barrier = pltpu.get_barrier_semaphore()

    def greet(peer):
        pl.semaphore_signal(barrier, inc=1, device_id={"row": peer})

    greet(fast)
    pl.when(has_slow)(lambda: greet(slow))
    greet(across)

    def level(k):
        return lax.rem(hi + k, quads) * 4 + me % 4

    for k in range(1, quads):
        greet(level(k))

    def lanes(start, size):
        return pl.ds(start, size) if isinstance(start, int) else pl.ds(pl.multiple_of(start, size), size)

    def halo_out(side, peer):
        src = lanes(side * hb, hb)
        there = 1 - side
        pairs = (
            (xyz_in.at[:, src], xyz_h.at[there]),
            (len_in.at[:, src], len_h.at[there]),
            (ids_in, ids_h.at[there]),
            (probes_in.at[:, src], probes.at[:, lanes(there * (own + hb), hb)]),
        )
        return [
            pltpu.make_async_remote_copy(
                src_ref=a, dst_ref=b, send_sem=halo_send.at[side, k], recv_sem=halo_recv.at[there, k],
                device_id={"row": peer},
            )
            for k, (a, b) in enumerate(pairs)
        ]

    def halo_arrival(side, peer):
        pairs = (
            (xyz_in.at[:, 0:hb], xyz_h.at[side]),
            (len_in.at[:, 0:hb], len_h.at[side]),
            (ids_in, ids_h.at[side]),
            (probes_in.at[:, 0:hb], probes.at[:, lanes(side * (own + hb), hb)]),
        )
        return [
            pltpu.make_async_remote_copy(
                src_ref=a, dst_ref=b, send_sem=halo_send.at[side, k], recv_sem=halo_recv.at[side, k],
                device_id={"row": peer},
            )
            for k, (a, b) in enumerate(pairs)
        ]

    slot = core * quads + hi

    def level_copies(k, source):
        at = core * quads + source
        return [
            pltpu.make_async_remote_copy(
                src_ref=fold_all.at[at], dst_ref=fold_all.at[at],
                send_sem=gat_send.at[k], recv_sem=gat_recv.at[k], device_id={"row": level(k)},
            ),
            pltpu.make_async_remote_copy(
                src_ref=cen_all.at[at], dst_ref=cen_all.at[at],
                send_sem=cen_send.at[k], recv_sem=cen_recv.at[k], device_id={"row": level(k)},
            ),
        ]

    def core_copies(which):
        held = pl.ds(which * quads, quads)
        return [
            pltpu.make_async_remote_copy(
                src_ref=fold_all.at[held], dst_ref=fold_all.at[held],
                send_sem=low_send.at[0], recv_sem=low_recv.at[0], device_id={"row": fast},
            ),
            pltpu.make_async_remote_copy(
                src_ref=cen_all.at[held], dst_ref=cen_all.at[held],
                send_sem=low_send.at[1], recv_sem=low_recv.at[1], device_id={"row": fast},
            ),
        ]

    center_copy = pltpu.make_async_remote_copy(
        src_ref=cen_all.at[slot], dst_ref=cen_y,
        send_sem=low_send.at[2], recv_sem=low_recv.at[2], device_id={"row": across},
    )
    sum_copy = pltpu.make_async_remote_copy(
        src_ref=red_out, dst_ref=red_in,
        send_sem=low_send.at[3], recv_sem=low_recv.at[3], device_id={"row": across},
    )

    def part_copy(side, x, peer, there=None):
        there = h * (1 - side) + x if there is None else there
        return pltpu.make_async_remote_copy(
            src_ref=acc.at[(ob + h) * side + x], dst_ref=part.at[there],
            send_sem=part_send.at[side * h + x], recv_sem=part_recv.at[there],
            device_id={"row": peer},
        )

    def slow_part(side, x):
        return part_copy(
            side, x, jnp.where(has_slow, slow, fast), jnp.where(has_slow, h * (1 - side) + x, ob + x)
        )

    def part_arrival(b, peer):
        return pltpu.make_async_remote_copy(
            src_ref=acc.at[b], dst_ref=part.at[b],
            send_sem=part_send.at[b], recv_sem=part_recv.at[b], device_id={"row": peer},
        )

    for load in loads[:2]:
        load.wait()
    row = lax.broadcasted_iota(jnp.int32, (ROWS, bs), 0)

    scale = jnp.where(row < 3, -2.0 * D_SCALE, jnp.where(row < 7, D_SCALE, 0.0))

    def fill_j(at, xyz, ln):
        rec_j[at, 0:3, :] = xyz
        rec_j[at, 3:6, :] = xyz
        rec_j[at, 6:7, :] = jnp.ones((1, bs), F32)
        rec_j[at, 7:8, :] = ln
        inv = 1.0 / ln
        scale_j[at] = scale * inv
        rhs_c[at] = right_stack((0.5 * C_SCALE) * jnp.where(row == 3, ln, jnp.where(row == 7, inv, 0.0)))

    lane = lax.broadcasted_iota(jnp.int32, (ROWS, 128), 1)
    own_centers = jnp.zeros((ROWS, 128), F32)
    for b in range(ob):
        ln = len_ref[:, b * bs : (b + 1) * bs]
        fill_j(h + b, xyz_ref[:, b * bs : (b + 1) * bs], ln)
        blk = rec_j[h + b]
        mean = jnp.sum(blk, axis=1, keepdims=True) * (1.0 / bs)
        own_centers = jnp.where(lane == b, mean, own_centers)
        cen = jnp.where(row < 6, jnp.broadcast_to(mean, (ROWS, bs)), 0.0)
        cen_j[b] = cen
        v = blk - cen
        norm = jnp.sum(jnp.where(row < 3, v * v, 0.0), axis=0, keepdims=True)
        feat = jnp.where(row < 3, v, jnp.where(row < 6, 1.0, norm)) * (1.0 / ln)
        lhs[b] = left_stack(jnp.where(row == 7, blk, feat)).T.astype(BF16)
    for load in loads[2:5]:
        load.wait()
    ids = ids_ref[...]
    slots = ids.shape[1]
    for b in range(ob):
        pb = probes[:, hb + b * bs : hb + (b + 1) * bs]
        fold = jnp.concatenate([nt(bin_ref[b, 0:half, :], pb), nt(bin_ref[b, half:, :], pb)], axis=1)
        fold_all[slot, b * half : (b + 1) * half, :] = fold.astype(BF16)
    square = jnp.concatenate([own_centers, jnp.zeros((128 - ROWS, 128), F32)], axis=0).T
    id_rows = jnp.concatenate(
        [jnp.zeros((ob, ROWS), F32), ids.astype(F32), jnp.zeros((ob, 128 - ROWS - slots), F32)], axis=1
    )
    own_cols = square[0:ob, :] + id_rows
    cen_all[slot] = own_cols

    def member(ids, target):
        return jnp.max(jnp.where(ids == target, 1.0, 0.0), axis=1, keepdims=True)

    gid = lax.broadcasted_iota(jnp.int32, ids.shape, 0) + me * ob

    def mask_at(offset, q):
        return (offset + HALO) * window + q

    for offset in range(-HALO, HALO + 1):
        wide = jnp.broadcast_to(member(ids, gid + offset), (ob, bs))
        for b in range(ob):
            mask[mask_at(offset, h + b)] = wide[b : b + 1, :]

    def right_side(o, q):
        v = rec_j[q] - cen_j[o]
        feat = jnp.where((row >= 3) & (row < 6), v * v, v) * scale_j[q]
        return jnp.concatenate([right_stack(feat), rhs_c[q]], axis=1)

    def entries(o, q, turn):
        both[turn] = nn(lhs[o], right_side(o, q))

    def values(turn, buf, s_at):
        for r in range(0, bs, STRIP):
            e = jnp.maximum(both[turn, r : r + STRIP, :bs], 1e-30)
            q = both[turn, r : r + STRIP, bs:]
            s = e * lax.rsqrt(e * q)
            buf[s_at, r : r + STRIP, :] = ((LOG2E + s) * jnp.exp2(-1.5 * lax.log2(q) - s)).astype(BF16)

    def add(at, value, seen):
        if at in seen:
            acc[at] += value
        else:
            acc[at] = value
            seen.add(at)

    def forward(o, q, buf, s, seen):
        p_q = probes[:, lanes(q * bs, bs)]
        add(h + o, mask[mask_at(q - h - o, h + o)] * nt(p_q, buf[s]), seen)

    def backward(o, q, buf, s, seen):
        if q != h + o:
            p_o = probes[:, lanes((h + o) * bs, bs)]
            add(q, mask[mask_at(h + o - q, q)] * nn(p_o, buf[s]), seen)

    def finish(pairs, t, keep, seen):
        if keep is None:
            forward(*pairs[t], value_buf, t % 2, seen)
            backward(*pairs[t], value_buf, t % 2, seen)
        else:
            backward(*pairs[t], kept, keep + t, seen)

    def sweep(pairs, seen, keep=None, old=None, after={}):
        entries(*pairs[0], 0)
        for t, pair in enumerate(pairs):
            if old:
                forward(*old[0][t], kept, old[1] + t, seen)
            if t + 1 < len(pairs):
                entries(*pairs[t + 1], (t + 1) % 2)
            if keep is None:
                values(t % 2, value_buf, t % 2)
            else:
                values(t % 2, kept, keep + t)
            if t:
                finish(pairs, t - 1, keep, seen)
                for hook in after.get(t - 1, ()):
                    hook()
        finish(pairs, len(pairs) - 1, keep, seen)
        for hook in after.get(len(pairs) - 1, ()):
            hook()

    table = []
    for g in range(h):
        c = [(s + g) // ob for s in range(ob + 1)]
        first = [g + k * (ob - 1 - 2 * g) for k in c]
        table.append([(f, h + f + s - k * (ob - g)) for s, (k, f) in enumerate(zip(c, first))])
    for g in range(h // 2):
        cols = [(g, ob), (h - 1 - g, h)]
        table.append([(i, h + ob + c) for c, stop in cols for i in range(c, stop)])
    for g in range(h // 2):
        table.append([(c, i - h) for i in (h + g, ob - 1 - g) for c in range(h // 2, i + 1)])

    left_groups = [(i, [(c, i) for c in range(h // 2, h + i + 1)]) for i in range(h)]
    right_groups = [(c, [(i, h + ob + c) for i in range(c, ob if c < h // 2 else h)]) for c in reversed(range(h))]
    right_groups.sort(key=lambda group: len(group[1]))
    slow_groups = (left_groups, right_groups)

    def open_links():
        pl.semaphore_wait(barrier, quads + 1 + jnp.where(has_slow, 1, 0))

        @pl.when(has_slow)
        def _():
            for copy in halo_out(side_slow, slow)[:3]:
                copy.start()

        for k in range(1, quads):
            for copy in level_copies(k, hi):
                copy.start()

        @pl.when(has_slow)
        def _():
            halo_out(side_slow, slow)[3].start()

        for copy in halo_out(side_fast, fast):
            copy.start()
        center_copy.start()

    def take_halo(side):
        first = side * (ob + h)
        for b in range(h):
            fill_j(first + b, xyz_h[side, :, b * bs : (b + 1) * bs], len_h[side, :, b * bs : (b + 1) * bs])
        there = ids_h[side]
        sign = 1 - 2 * side
        base = gid + (2 * side - 1) * ob
        for dj in range(1, HALO + 1):
            wide = jnp.broadcast_to(member(there, base + sign * dj), (ob, bs))
            for b in range(h):
                mask[mask_at(sign * dj, first + b)] = wide[(1 - side) * h + b : (1 - side) * h + b + 1, :]

    def take_fast(side):
        for copy in halo_arrival(side, fast):
            copy.wait_recv()
        take_halo(side)

    def take_slow(side):
        @pl.when(has_slow)
        def _():
            for copy in halo_arrival(side, slow)[:3]:
                copy.wait_recv()

        @pl.when(jnp.logical_not(has_slow))
        def _():
            xyz_h[side] = xyz_ref[:, 0:hb]
            len_h[side] = len_ref[:, 0:hb]
            ids_h[side] = ids_ref[...]
            probes[:, lanes(side * (own + hb), hb)] = probes[:, hb : 2 * hb]

        take_halo(side)

    def take_slow_probes(side):
        @pl.when(has_slow)
        def _():
            halo_arrival(side, slow)[3].wait_recv()

    def level_done():
        for k in range(1, quads):
            for copy in level_copies(k, hi):
                copy.wait()
        for copy in core_copies(core):
            copy.start()

    step_w = min(128, width)

    def partial_sums():
        for copy in core_copies(core):
            copy.wait()
        center_copy.wait()
        centers = cen_all[...].reshape(width, 128).T
        mine = cen_all[slot]
        column = lax.broadcasted_iota(jnp.int32, (ob, width), 1)
        holder = column // ob
        device = holder % quads * 4 + col_y * 2 + holder // quads
        global_ids = (device * ob + column % ob).astype(F32)
        picks = (0, 1, 2, 7)
        pick_r = lax.broadcasted_iota(jnp.int32, (step_w, step_w * half), 0)
        pick_c = lax.broadcasted_iota(jnp.int32, (step_w, step_w * half), 1)
        spread = jnp.where(pick_c // half == pick_r, 1.0, 0.0).astype(BF16)
        eye_r = lax.broadcasted_iota(jnp.int32, (ob * half, step_w * half), 0)
        eye_c = lax.broadcasted_iota(jnp.int32, (ob * half, step_w * half), 1)
        same = lax.rem(eye_r, half) == lax.rem(eye_c, half)
        per = step_w // ob
        for rows, target in ((cen_y[...], red_out), (mine, own_sum)):
            coupling = matern([rows[:, c : c + 1] for c in picks], [centers[c : c + 1, :] for c in picks])
            near = jnp.zeros((ob, width), F32)
            for t in range(slots):
                near = jnp.where(rows[:, ROWS + t : ROWS + t + 1] == global_ids, 1.0, near)
            coupling = jnp.where(near > 0.0, 0.0, coupling).astype(BF16)
            total = jnp.zeros((ob * half, 2 * np_), F32)
            for q in range(width // step_w):
                wide = nn(coupling[:, q * step_w : (q + 1) * step_w], spread)
                wide = jnp.concatenate(
                    [jnp.broadcast_to(wide[i : i + 1, :], (half, step_w * half)) for i in range(ob)], axis=0
                )
                kron = jnp.where(same, wide, 0.0).astype(BF16)
                folded = fold_all[q * per : (q + 1) * per].reshape(step_w * half, 2 * np_)
                total = total + nn(kron, folded)
            target[...] = total
            if target is red_out:
                sum_copy.start()

    before = min(BEFORE, h)
    there = before + h // 2

    def rest(mine):
        at_slow = mine
        at_fast = 1 - mine
        seen = set(touched)

        slow_tiles = [tile for _, tiles in slow_groups[at_slow] for tile in tiles]

        def cross_tiles(side, k):
            return table[h + k] if side else table[h + h // 2 + k]

        for t in range(before, ob):
            if t == before:
                take_slow(at_slow)
                after, count = {}, 0
                for x, tiles in slow_groups[at_slow]:
                    count += len(tiles)
                    after[count - 1] = [lambda x=x: slow_part(at_slow, x).start()]
                after.setdefault(min(LEVEL_TILE, count - 1), []).append(level_done)
                sweep(slow_tiles, seen, keep=0, after=after)
            if t == there:
                take_slow_probes(at_slow)
                take_fast(at_fast)
            if t >= there:
                if t < before + h:
                    k = t - there
                    at = k * (ob + 1)
                    after = {min(SUM_TILE, ob): [partial_sums]} if k == 0 else {}
                    sweep(cross_tiles(at_fast, k), seen, old=(slow_tiles[at : at + ob + 1], at), after=after)
                    part_copy(at_fast, k, fast).start()
                    part_copy(at_fast, h - 1 - k, fast).start()
                else:
                    sweep(table[t - h], seen)

    early = [tile for tiles in table[:before] for tile in tiles]
    touched = set()
    sweep(early[:OPEN_TILE], touched)
    open_links()
    sweep(early[OPEN_TILE:], touched)
    for c in range(2):
        pl.when(core == c)(functools.partial(rest, c))

    loads[5].wait()

    for x in range(h):
        part_arrival(side_fast * h + x, fast).wait_recv()

    @pl.when(has_slow)
    def _():
        for x in range(h):
            part_arrival(side_slow * h + x, slow).wait_recv()

    @pl.when(jnp.logical_not(has_slow))
    def _():
        for x in range(h):
            part[side_slow * h + x] = jnp.zeros((np_, bs), F32)

    for b in range(ob):
        out_ref[:, b * bs : (b + 1) * bs] = acc[h + b] + part[b]

    sum_copy.wait()
    summed = (own_sum[...] + red_in[...]).astype(BF16)
    for b in range(ob):
        mine = summed[b * half : (b + 1) * half, :]
        far = tn(mine[:, :np_], bout_ref[b, 0:half, :]) + tn(mine[:, np_:], bout_ref[b, half:, :])
        out_ref[:, b * bs : (b + 1) * bs] += far

    for copy in halo_out(side_fast, fast):
        copy.wait_send()
    for x in range(h):
        part_copy(side_fast, x, fast).wait_send()

    @pl.when(has_slow)
    def _():
        for copy in halo_out(side_slow, slow):
            copy.wait_send()

    for x in range(h):
        slow_part(side_slow, x).wait_send()

    @pl.when(jnp.logical_or(me == 1, me == n - 2))
    def _():
        for x in range(h):
            part_arrival(ob + x, fast).wait_recv()


def solution(mesh):
    n = mesh.shape["row"]

    def shards(coordinates, length_scale, probes, near_ids, near_count, basis_out, basis_in):
        ob, rank, bs = basis_out.shape
        np_ = probes.shape[0]
        own = ob * bs
        h = ob // 2
        slots = near_ids.shape[1]
        window = ob + 2 * h
        vmem = pl.BlockSpec(memory_space=pltpu.VMEM)
        dma = pltpu.SemaphoreType.DMA
        return pl.pallas_call(
            functools.partial(kernel, n, ob, bs),
            out_shape=jax.ShapeDtypeStruct((np_, own), F32),
            in_specs=[pl.BlockSpec(memory_space=pl.ANY)] * 6,
            out_specs=vmem,
            scratch_shapes=[
                pltpu.VMEM((3, own), F32),
                pltpu.VMEM((1, own), F32),
                pltpu.VMEM((ob, slots), jnp.int32),
                pltpu.VMEM((ob, rank, bs), BF16),
                pltpu.VMEM((ob, rank, bs), BF16),
                pltpu.VMEM((2, 3, h * bs), F32),
                pltpu.VMEM((2, 1, h * bs), F32),
                pltpu.VMEM((2, ob, slots), jnp.int32),
                pltpu.VMEM((np_, window * bs), BF16),
                pltpu.VMEM((window, ROWS, bs), F32),
                pltpu.VMEM((window, ROWS, bs), F32),
                pltpu.VMEM((ob, ROWS, bs), F32),
                pltpu.VMEM((ob, bs, 8 * ROWS), BF16),
                pltpu.VMEM((window, 8 * ROWS, bs), BF16),
                pltpu.VMEM(((2 * HALO + 1) * window, 1, bs), F32),
                pltpu.VMEM((window, np_, bs), F32),
                pltpu.VMEM((ob + h, np_, bs), F32),
                pltpu.VMEM((n // 2, ob * rank // 2, 2 * np_), BF16),
                pltpu.VMEM((n // 2, ob, 128), F32),
                pltpu.VMEM((ob, 128), F32),
                pltpu.VMEM((ob * rank // 2, 2 * np_), F32),
                pltpu.VMEM((ob * rank // 2, 2 * np_), F32),
                pltpu.VMEM((ob * rank // 2, 2 * np_), F32),
                pltpu.VMEM((2, bs, 2 * bs), F32),
                pltpu.VMEM((2, bs, bs), BF16),
                pltpu.VMEM((h // 2 * (ob + 1), bs, bs), BF16),
                dma((6,)), dma((2, 4)), dma((2, 4)), dma((ob + h,)), dma((ob + h,)),
                dma((n // 4,)), dma((n // 4,)), dma((n // 4,)), dma((n // 4,)), dma((4,)), dma((4,)),
            ],
            compiler_params=pltpu.CompilerParams(collective_id=0, has_side_effects=True, vmem_limit_bytes=16 * 1024 * 1024),
        )(
            *[
                pltpu.with_memory_space_constraint(x, pltpu.HBM)
                for x in (coordinates, length_scale.reshape(1, own), probes, near_ids, basis_out, basis_in)
            ]
        )

    placed = (
        P(None, ("grp", "row")),
        P(("grp", "row")),
        P(None, ("grp", "row")),
        P(("grp", "row"), None),
        P(("grp", "row")),
        P(("grp", "row"), None, None),
        P(("grp", "row"), None, None),
    )
    return jax.shard_map(
        shards, mesh=mesh, in_specs=placed, out_specs=P(None, ("grp", "row")), check_vma=False
    )
```
